32 devices in a mesh: jet: 8 (over z, y), grp: 4 (over x, core).
Axes of the slice: x: 2, y: 2, z: 4, core: 2. Of those that a mesh axis runs over, the one named last changes fastest.
Arguments:
- sources: float32 [3, 24, 192, 384], P(None, 'jet', 'grp'), may hold values from -8 to 8
- cotangent: float32 [3, 24, 192, 384], P(None, 'jet', 'grp'), may hold values from -6 to 6
- width_class: int32 [24, 192, 3], P('jet', 'grp'), may hold values from 0 to 7
Outputs:
- filtered: float32 [3, 24, 192, 384], P(None, 'jet', 'grp')
- adjoint: float32 [3, 24, 192, 384], P(None, 'jet', 'grp')
The draws below stay inside these ranges and needn't reach their ends.
All inputs are finite; a program needn't handle non-finite values.
Results may differ from the reference program's by a relative error of at most 0.00002.
Values sent between devices are 32-bit elements; how exact they have to be, the bound alone decides.
No kernel may reach another device: no remote copies, remote signals or barrier semaphores. Data moves between devices by JAX's collectives and lax.ppermute only.
A program may use at most 128 MiB of HBM per device.

```python
import jax
import jax.numpy as jnp
from jax import lax

NY = 384
BLOCK = 128
CLASSES = 8
COARSE_SWEEPS = 8
NZ = 24
NX = 192


def draw_sources(key, part):
    shape = (3, NZ, NX, NY)
    return jnp.clip(2.0 * jax.random.normal(key, shape, jnp.float32), -8.0, 8.0)


def with_ends(values, key, smallest, largest):
    index_at = [jax.random.randint(jax.random.fold_in(key, axis), (), 0, length) for axis, length in enumerate(values.shape)]
    longest = values.shape.index(max(values.shape))
    neighbour = index_at[:longest] + [(index_at[longest] + 1) % values.shape[longest]] + index_at[longest + 1:]
    return values.at[tuple(index_at)].set(smallest).at[tuple(neighbour)].set(largest)


def steps_of(rng, dims, split, smallest, largest):
    def one(position, shards_of):
        steps = jax.random.uniform(jax.random.fold_in(jax.random.fold_in(rng, 6), position), (shards_of,), jnp.float32, smallest / len(split), largest / len(split))
        return jnp.repeat(jnp.exp(steps), dims[position] // shards_of).reshape((-1,) + (1,) * (len(dims) - position - 1))

    loudness = one(*split[0])
    for cut in split[1:]:
        loudness = loudness * one(*cut)
    return loudness


def scatter_about(own_key, extent, spread, bound, split=(), held_as=jnp.bfloat16):
    level = steps_of(own_key, extent, split, -0.22, 0.18) if split else 1.0
    result = jax.random.normal(own_key, extent, jnp.float32) * spread * level
    return jnp.minimum(jnp.maximum(result, -bound), bound).astype(held_as)


def setup_inputs(seed: int = 0) -> dict:
    keys = jax.random.split(jax.random.key(seed), 4)
    return {
        "sources": draw_sources(jax.random.fold_in(keys[3], 71), 0),
        "cotangent": scatter_about(keys[1], (3, NZ, NX, NY), 1.0, 6.0, ((1, 8), (2, 4)), jnp.float32),
        "width_class": with_ends(jax.random.randint(keys[2], (NZ, NX, NY // BLOCK), 0, CLASSES), jax.random.fold_in(keys[2], 1), 0, CLASSES - 1).astype(jnp.int32),
    }


WIDTH_TABLE = (2.5, 3.5, 4.5, 5.0, 6.0, 7.0, 8.5, 10.0)
RELAXATION = 0.8
COARSE_RELAX = 0.8

def width_field(width_class):
    table = jnp.array(WIDTH_TABLE, jnp.float32)
    table = table * table / 24.0
    hits = (width_class[..., None] == jnp.arange(CLASSES, dtype=jnp.int32)).astype(jnp.float32)
    blocks = lax.optimization_barrier(jnp.sum(hits * table, axis=-1))
    return jnp.repeat(blocks, BLOCK, axis=-1)

def face_coefs(kappa):
    padded = jnp.pad(kappa, 1)
    return ((kappa + padded[:-2, 1:-1, 1:-1]) * 0.5, (kappa + padded[2:, 1:-1, 1:-1]) * 0.5, (kappa + padded[1:-1, :-2, 1:-1]) * 0.5, (kappa + padded[1:-1, 2:, 1:-1]) * 0.5, (kappa + padded[1:-1, 1:-1, :-2]) * 0.5, (kappa + padded[1:-1, 1:-1, 2:]) * 0.5)

def operate(field, faces, diagonal):
    padded = jnp.pad(field, ((0, 0), (1, 1), (1, 1), (1, 1)))
    nearby = faces[0] * padded[:, :-2, 1:-1, 1:-1] + faces[1] * padded[:, 2:, 1:-1, 1:-1]
    nearby = nearby + faces[2] * padded[:, 1:-1, :-2, 1:-1] + faces[3] * padded[:, 1:-1, 2:, 1:-1]
    nearby = nearby + faces[4] * padded[:, 1:-1, 1:-1, :-2] + faces[5] * padded[:, 1:-1, 1:-1, 2:]
    return diagonal * field - nearby

def restrict(field):
    shape = field.shape
    blocks = field.reshape(shape[:-2] + (shape[-2] // 4, 4, shape[-1] // 4, 4))
    return lax.optimization_barrier(jnp.mean(blocks, axis=(-3, -1)))

def prolong(field):
    return jnp.repeat(jnp.repeat(field, 4, axis=-2), 4, axis=-1)

def coarse_solve(coarse_res, coarse_kappa):
    padded = jnp.pad(coarse_kappa, ((0, 0), (1, 1), (1, 1)))
    faces = ((coarse_kappa + padded[:, :-2, 1:-1]) * 0.5, (coarse_kappa + padded[:, 2:, 1:-1]) * 0.5, (coarse_kappa + padded[:, 1:-1, :-2]) * 0.5, (coarse_kappa + padded[:, 1:-1, 2:]) * 0.5)
    coarse_diag = 1.0 + faces[0] + faces[1] + faces[2] + faces[3]
    coarse_inv = COARSE_RELAX / coarse_diag
    estimate = coarse_inv * coarse_res
    for number in range(COARSE_SWEEPS - 1):
        epad = jnp.pad(estimate, ((0, 0), (0, 0), (1, 1), (1, 1)))
        nearby = faces[0] * epad[:, :, :-2, 1:-1] + faces[1] * epad[:, :, 2:, 1:-1]
        nearby = nearby + faces[2] * epad[:, :, 1:-1, :-2] + faces[3] * epad[:, :, 1:-1, 2:]
        applied = coarse_diag * estimate - nearby
        estimate = estimate + coarse_inv * (coarse_res - applied)
    plane = lax.optimization_barrier(jnp.sum(coarse_res, axis=(-2, -1))) / lax.optimization_barrier(jnp.sum(coarse_diag, axis=(-2, -1)))
    return estimate + plane[..., None, None]

def reference(sources, cotangent, width_class):
    kappa = width_field(width_class)
    faces = face_coefs(kappa)
    diagonal = 1.0 + faces[0] + faces[1] + faces[2] + faces[3] + faces[4] + faces[5]
    inverse = RELAXATION / diagonal
    coarse_kappa = restrict(kappa) / 16.0

    def cycle(source):
        field = inverse * source
        for number in range(2):
            field = field + inverse * (source - operate(field, faces, diagonal))
        resid = source - operate(field, faces, diagonal)
        field = field + prolong(coarse_solve(restrict(resid), coarse_kappa))
        field = field + inverse * (source - operate(field, faces, diagonal))
        return field
    filtered, pullback = jax.vjp(cycle, sources)
    adjoint = pullback(cotangent)[0]
    return (filtered, adjoint)
```

```python
import functools

import jax
import jax.numpy as jnp
from jax import lax
from jax.experimental import pallas as pl
from jax.experimental.pallas import tpu as pltpu
from jax.sharding import PartitionSpec as P

BLOCK = 128
CLASSES = 8
COARSE_SWEEPS = 8
DEEP = 3
O = 16
LO = 8
WIDTH_TABLE = (2.5, 3.5, 4.5, 5.0, 6.0, 7.0, 8.5, 10.0)
RELAXATION = 0.8
COARSE_RELAX = 0.8
F32 = jnp.float32
HI = lax.Precision.HIGHEST


VM = pl.BlockSpec(memory_space=pltpu.VMEM)
SM = pl.BlockSpec(memory_space=pltpu.SMEM)


def call(kernel, outs, scratch, *args, smem=0, cost=(1000000, 1000000)):
    specs = [SM] * smem + [VM] * (len(args) - smem)
    return pl.pallas_call(
        kernel,
        out_shape=[jax.ShapeDtypeStruct(s, F32) for s in outs],
        in_specs=specs,
        out_specs=[VM] * len(outs),
        scratch_shapes=[pltpu.VMEM(s, F32) for s in scratch],
        cost_estimate=pl.CostEstimate(flops=cost[0], bytes_accessed=cost[1], transcendentals=0),
        compiler_params=pltpu.CompilerParams(vmem_limit_bytes=60 << 20),
    )(*args)


def iota(shape, dim):
    return lax.broadcasted_iota(jnp.int32, shape, dim)


def pack_x(f, g, ks, up, dn):
    nf, nz, nx, _ = f.shape
    up[...] = jnp.zeros_like(up)
    dn[...] = jnp.zeros_like(dn)
    for s, ref in enumerate((f, g)):
        for a in range(nf):
            for p in range(nz):
                at = ((s * nf + a) * nz + p) * DEEP
                up[at:at + DEEP, :] = ref[a, p, nx - DEEP:nx, :]
                dn[at:at + DEEP, :] = ref[a, p, 0:DEEP, :]
    at = kappa_row(nf, nz)
    up[at:at + 4, 0:BLOCK] = ks[nx - 4:nx, :]
    dn[at:at + 4, 0:BLOCK] = ks[0:4, :]


def kappa_row(nf, nz):
    return -(-2 * nf * nz * DEEP // 8) * 8


def pack_y(low, high, ks, out, ksx, *, nf, nz, nx):
    out[...] = jnp.zeros_like(out)
    for a in range(2 * nf):
        for p in range(nz):
            src = (a * nz + p) * DEEP
            at = (a * nz + p) * 4
            out[at:at + 2, :] = low[src + 1:src + 3, :]
            out[at + 2:at + 4, :] = high[src:src + 2, :]
    kr = kappa_row(nf, nz)
    ksx[0:4, :] = low[kr:kr + 4, 0:BLOCK]
    ksx[4:4 + nx, :] = ks[...]
    ksx[4 + nx:8 + nx, :] = high[kr:kr + 4, 0:BLOCK]


def around(v, b, nb, lane):
    rl = [pltpu.roll(x, 1, 1) for x in v]
    rr = [pltpu.roll(x, BLOCK - 1, 1) for x in v]
    left = [jnp.where(lane == 0, rl[i - 1] if i > 0 else 0.0, rl[i]) for i in range(nb)]
    right = [jnp.where(lane == BLOCK - 1, rr[i + 1] if i < nb - 1 else 0.0, rr[i]) for i in range(nb)]
    return left, right


def pull(src, co, p, q, r, a, nb, lane):
    czm, czp, cxm, cxp, cym, cyp = co
    v = [src[a, q, b, r:r + 8, :] for b in range(nb)]
    left, right = around(v, None, nb, lane)
    out = []
    for b in range(nb):
        s = czm[b] * src[a, q - 1, b, r:r + 8, :] + czp[b] * src[a, q + 1, b, r:r + 8, :]
        s = s + cxm[b] * src[a, q, b, r - 1:r + 7, :] + cxp[b] * src[a, q, b, r + 1:r + 9, :]
        s = s + cym[b] * left[b] + cyp[b] * right[b]
        out.append(s)
    return v, out


def coefs_at(cz, cx, cm, cp, p, r, nb):
    return (
        [cz[p, b, r:r + 8, :] for b in range(nb)],
        [cz[p + 1, b, r:r + 8, :] for b in range(nb)],
        [cx[p, b, r - 1:r + 7, :] for b in range(nb)],
        [cx[p, b, r:r + 8, :] for b in range(nb)],
        [cm[p, b, r:r + 8, :] for b in range(nb)],
        [cp[p, b, r:r + 8, :] for b in range(nb)],
    )


def rows_of(wide, nx):
    return range(LO, LO + nx + 16, 8) if wide else range(O, O + nx, 8)


def sweep(dst, src, rhs, coef, first, planes, wide, nx, doff=0, roff=0, soff=0):
    cz, cx, cm, cp, inv = coef
    nf, nb = src.shape[0], src.shape[2]
    lane = iota((8, BLOCK), 1)

    def plane(i, _):
        p = first + i * planes[1]
        for r in rows_of(wide, nx):
            co = coefs_at(cz, cx, cm, cp, p, r, nb)
            w = [inv[p, b, r:r + 8, :] for b in range(nb)]
            for a in range(nf):
                v, s = pull(src, co, p, p - soff, r, a, nb, lane)
                for b in range(nb):
                    dst[a, p - doff, b, r - (0 if doff < 100 else 0):r + 8, :] = (
                        (1.0 - RELAXATION) * v[b] + w[b] * (rhs[a, p - roff, b, r:r + 8, :] + s[b]))
        return 0

    lax.fori_loop(0, planes[0], plane, 0)


def restrict_residual(out, at, src, rhs, coef, diag, tmp, lanes, nz, nx):
    cz, cx, cm, cp, _ = coef
    nf, nb = src.shape[0], src.shape[2]
    lane = iota((8, BLOCK), 1)

    def plane(i, _):
        p = DEEP + i
        for r in rows_of(False, nx):
            co = coefs_at(cz, cx, cm, cp, p, r, nb)
            d = [diag[i, b, r:r + 8, :] for b in range(nb)]
            for a in range(nf):
                v, s = pull(src, co, p, p, r, a, nb, lane)
                for b in range(nb):
                    tmp[a * nz + i, b, r - O:r - O + 8, :] = rhs[a, p, b, r:r + 8, :] - d[b] * v[b] + s[b]
        return 0

    lax.fori_loop(0, nz, plane, 0)
    nc = nx // 4
    for k in range(nf * nz):
        total = None
        for b in range(nb):
            part = sum(tmp[k, b, pl.ds(j, nc, stride=4), :] for j in range(4))
            dot = jnp.dot(part, lanes[b], precision=HI, preferred_element_type=F32)
            total = dot if total is None else total + dot
        out[at + k * nc:at + (k + 1) * nc, :] = total


def lane_sum(nb):
    l, m = iota((BLOCK, BLOCK), 0), iota((BLOCK, BLOCK), 1)
    return [jnp.where((l + b * BLOCK) // 4 == m, 1.0 / 16.0, 0.0).astype(F32) for b in range(nb)]


def lane_copy(b):
    m, l = iota((BLOCK, BLOCK), 0), iota((BLOCK, BLOCK), 1)
    return jnp.where((l + b * BLOCK) // 4 == m, 1.0, 0.0).astype(F32)


def before(info, f, g, pf, pg, rf, rg, low, high, py, ry, ksx, pks, rks, kdn, kup,
           u3, gx, cz, cx, cm, cp, inv, rc, fx, ua, ub, kap, diag, tmp):
    nf, nz, nx, ny = f.shape
    nb = ny // BLOCK
    par, first_j, last_j, first_g, last_g = (info[i] for i in range(5))
    for ref in (fx, gx, kap, ua, ub, cx):
        ref[...] = jnp.zeros_like(ref)
    pbase = jnp.where(par == 0, 2 * nz, 0)
    rbase = 2 * nz - pbase
    for s, (dst, own, part, rel) in enumerate(((fx, f, pf, rf), (gx, g, pg, rg))):
        for a in range(nf):
            for p in range(nz):
                for b in range(nb):
                    c = slice(b * BLOCK, (b + 1) * BLOCK)
                    dst[a, nz + p, b, O:O + nx, :] = own[a, p, :, c]
                    dst[a, pbase + p, b, O:O + nx, :] = part[a, p, :, c]
                    dst[a, rbase + p, b, O:O + nx, :] = rel[a, p, :, c]
                    at = ((s * nf + a) * nz + p) * DEEP
                    dst[a, nz + p, b, O - DEEP:O, :] = low[at:at + DEEP, c]
                    dst[a, nz + p, b, O + nx:O + nx + DEEP, :] = high[at:at + DEEP, c]
                    at = ((s * nf + a) * nz + p) * 4
                    dst[a, pbase + p, b, O - 2:O, :] = py[at:at + 2, c]
                    dst[a, pbase + p, b, O + nx:O + nx + 2, :] = py[at + 2:at + 4, c]
                    dst[a, rbase + p, b, O - 2:O, :] = ry[at:at + 2, c]
                    dst[a, rbase + p, b, O + nx:O + nx + 2, :] = ry[at + 2:at + 4, c]
    for p in range(nz):
        for b in range(nb):
            c = p * nb + b
            for base, ref in ((1 + nz, ksx), (1 + pbase, pks), (1 + rbase, rks)):
                kap[base + p, b, O - 4:O + nx + 4, :] = jnp.broadcast_to(ref[:, c:c + 1], (nx + 8, BLOCK))
    for b in range(nb):
        c = (nz - 1) * nb + b
        kap[0, b, O - 4:O + nx + 4, :] = jnp.broadcast_to(kup[:, c:c + 1], (nx + 8, BLOCK))
        kap[3 * nz + 1, b, O - 4:O + nx + 4, :] = jnp.broadcast_to(kdn[:, b:b + 1], (nx + 8, BLOCK))
    span = slice(LO, LO + nx + 16)
    n = nx + 16
    lane = iota((n, BLOCK), 1)
    row = iota((n, BLOCK), 0) + (LO - O)
    inside = jnp.where(((row < 0) & (first_g == 1)) | ((row >= nx) & (last_g == 1)), 0.0, RELAXATION)

    def cplane(p, _):
        out = ((first_j == 1) & (p < nz)) | ((last_j == 1) & (p >= 2 * nz))
        here = inside * jnp.where(out, 0.0, 1.0)
        k = [kap[p + 1, b, span, :] for b in range(nb)]
        for b in range(nb):
            zm = 0.5 * (kap[p, b, span, :] + k[b])
            zp = 0.5 * (k[b] + kap[p + 2, b, span, :])
            xp = 0.5 * (k[b] + kap[p + 1, b, LO + 1:LO + n + 1, :])
            xm = 0.5 * (k[b] + kap[p + 1, b, LO - 1:LO + n - 1, :])
            ym = jnp.where(lane == 0, 0.5 * (k[b] + k[b - 1]) if b > 0 else 0.5 * k[b], k[b])
            yp = jnp.where(lane == BLOCK - 1, 0.5 * (k[b] + k[b + 1]) if b < nb - 1 else 0.5 * k[b], k[b])
            cz[p, b, span, :] = zm
            cz[p + 1, b, span, :] = zp
            cx[p, b, span, :] = xp
            cm[p, b, span, :] = ym
            cp[p, b, span, :] = yp
            d = 1.0 + zm + zp + xm + xp + ym + yp
            w = here / d
            inv[p, b, span, :] = w

            @pl.when((p >= nz) & (p < 2 * nz))
            def _():
                diag[p - nz, b, span, :] = d
            for a in range(nf):
                ua[a, p, b, span, :] = w * fx[a, p, b, span, :]
        return 0

    lax.fori_loop(0, 3 * nz, cplane, 0)
    coef = (cz, cx, cm, cp, inv)
    lanes = lane_sum(nb)
    sweep(ub, ua, fx, coef, 2, (2 * nz - 1, 1), True, nx)
    sweep(ub, ua, fx, coef, 1, (2, 3 * nz - 3), False, nx)
    sweep(ua, ub, fx, coef, nz, (nz, 1), True, nx)
    sweep(ua, ub, fx, coef, nz - 1, (2, nz + 1), False, nx)
    restrict_residual(rc, 0, ua, fx, coef, diag, tmp, lanes, nz, nx)
    for a in range(nf):
        u3[a] = ua[a, nz - 1:2 * nz + 1]

    def gplane(i, _):
        p = nz - 1 + i
        for b in range(nb):
            w = inv[p, b, span, :]
            for a in range(nf):
                ua[a, p, b, span, :] = w * gx[a, p, b, span, :]
        return 0

    lax.fori_loop(0, nz + 2, gplane, 0)
    nc = nx // 4
    restrict_residual(rc, nf * nz * nc, ua, gx, coef, diag, tmp, lanes, nz, nx)
    for p in range(nz):
        tmp[p, 0, 0:nx, :] = ksx[4:4 + nx, :]
        kc = sum(tmp[p, 0, pl.ds(j, nc, stride=4), :] for j in range(4)) * (1.0 / 64.0)
        l, m = iota((BLOCK, BLOCK), 0), iota((BLOCK, BLOCK), 1)
        pick = jnp.where((l - p * nb == m - (BLOCK - nb)) & (m >= BLOCK - nb), 1.0, 0.0).astype(F32)
        rows = slice(p * nc, (p + 1) * nc)
        rc[rows, :] = rc[rows, :] + jnp.dot(kc, pick, precision=HI, preferred_element_type=F32)


def coarse(info, rc, est, msg_up, msg_dn, full, e0, e1, ck, cf, *, nf, nz, ng, nc, nb):
    k2 = 2 * nf
    nr = ng * nc
    per = k2 * nz * nc
    lane = iota((nr, BLOCK), 1)
    used = BLOCK // 4 * nb
    e0[...] = jnp.zeros_like(e0)
    e1[...] = jnp.zeros_like(e1)
    ck[...] = jnp.zeros_like(ck)
    g = info[5]
    start = g * nc
    for k in range(k2 * nz):
        for i in range(ng):
            full[k, i * nc:(i + 1) * nc, :] = rc[i * per + k * nc:i * per + (k + 1) * nc, :]
    for p in range(nz):
        raw = full[p]
        kc = jnp.zeros((nr, BLOCK), F32)
        for b in range(nb):
            column = jnp.broadcast_to(raw[:, BLOCK - nb + b:BLOCK - nb + b + 1], (nr, BLOCK))
            kc = jnp.where(lane // (BLOCK // 4) == b, column, kc)
        ck[p, 8:8 + nr, :] = kc
        full[p] = jnp.where(lane < used, raw, 0.0)
    m = iota((16, nr), 0)
    q = iota((16, nr), 1)
    rows = jnp.where(q == m + start - 1, 1.0, 0.0).astype(F32)
    for p in range(nz):
        k = ck[p, 8:8 + nr, :]
        valid = lane < used
        xm = jnp.where(valid, 0.5 * (k + ck[p, 7:7 + nr, :]), 0.0)
        xp = jnp.where(valid, 0.5 * (k + ck[p, 9:9 + nr, :]), 0.0)
        ym = jnp.where(valid, 0.5 * (k + pltpu.roll(k, 1, 1)), 0.0)
        yp = jnp.where(valid, 0.5 * (k + pltpu.roll(k, BLOCK - 1, 1)), 0.0)
        d = jnp.where(valid, 1.0 + xm + xp + ym + yp, 0.0)
        ci = jnp.where(valid, COARSE_RELAX / jnp.where(valid, d, 1.0), 0.0)
        cf[0] = xm
        cf[1] = xp
        cf[2] = ym
        cf[3] = yp
        cf[4] = ci
        dsum = jnp.sum(d)
        for a in range(k2):
            e0[a, 8:8 + nr, :] = ci * full[a * nz + p]

        def step(src, dst):
            for r in range(0, nr, 8):
                s8 = slice(r, r + 8)
                c = [cf[i, s8, :] for i in range(5)]
                for a in range(k2):
                    v = src[a, 8 + r:16 + r, :]
                    s = c[0] * src[a, 7 + r:15 + r, :] + c[1] * src[a, 9 + r:17 + r, :]
                    s = s + c[2] * pltpu.roll(v, 1, 1) + c[3] * pltpu.roll(v, BLOCK - 1, 1)
                    dst[a, 8 + r:16 + r, :] = (1.0 - COARSE_RELAX) * v + c[4] * (full[a * nz + p, s8, :] + s)

        for i in range(COARSE_SWEEPS - 1):
            step(*((e0, e1) if i % 2 == 0 else (e1, e0)))
        last = e1 if (COARSE_SWEEPS - 1) % 2 else e0
        for a in range(k2):
            shift = jnp.sum(full[a * nz + p]) / dsum
            done = jnp.where(valid, last[a, 8:8 + nr, :] + shift, 0.0)
            own = jnp.dot(rows, done, precision=HI, preferred_element_type=F32)
            k = a * nz + p
            est[k * 16:(k + 1) * 16, :] = own
            msg_up[k * 16:(k + 1) * 16, :] = own
            msg_dn[k * 16:(k + 1) * 16, :] = own


def after(info, f, u3, gx, cz, cx, cm, cp, inv, est, elo, ehi, filtered, adjoint, ua, ub, cpad):
    nf, nz, nx, ny = f.shape
    nb = ny // BLOCK
    nc = nx // 4
    coef = (cz, cx, cm, cp, inv)
    span = slice(LO, LO + nx + 16)
    copies = [lane_copy(b) for b in range(nb)]

    def prolong(ref, k, b):
        e = jnp.dot(ref[k * 16:(k + 1) * 16, :], copies[b], precision=HI, preferred_element_type=F32)
        for j in range(4):
            cpad[pl.ds(O - 4 + j, nc + 2, stride=4), :] = e[0:nc + 2, :]
        return cpad[span, :]

    cpad[...] = jnp.zeros_like(cpad)
    ua[...] = jnp.zeros_like(ua)
    ub[...] = jnp.zeros_like(ub)
    for a in range(nf):
        for i in range(nz + 2):
            ref, p = (elo, nz - 1) if i == 0 else ((ehi, 0) if i == nz + 1 else (est, i - 1))
            for b in range(nb):
                ua[a, nz - 1 + i, b, span, :] = u3[a, i, b, span, :] + prolong(ref, a * nz + p, b)
    lane = iota((8, BLOCK), 1)

    def last(dst, src, rhs):
        def plane(i, _):
            p = nz + i
            for r in rows_of(False, nx):
                co = coefs_at(cz, cx, cm, cp, p, r, nb)
                w = [inv[p, b, r:r + 8, :] for b in range(nb)]
                for a in range(nf):
                    v, s = pull(src, co, p, p, r, a, nb, lane)
                    for b in range(nb):
                        dst[a, i, r - O:r - O + 8, b * BLOCK:(b + 1) * BLOCK] = (
                            (1.0 - RELAXATION) * v[b] + w[b] * (rhs(a, i, b, r) + s[b]))
            return 0

        lax.fori_loop(0, nz, plane, 0)

    last(filtered, ua, lambda a, i, b, r: f[a, i, r - O:r - O + 8, b * BLOCK:(b + 1) * BLOCK])
    for a in range(nf):
        for i in range(3 * nz):
            ref = elo if i < nz else (ehi if i >= 2 * nz else est)
            for b in range(nb):
                ua[a, i, b, span, :] = inv[i, b, span, :] * gx[a, i, b, span, :] + prolong(ref, (nf + a) * nz + i % nz, b)
    sweep(ub, ua, gx, coef, 2, (2 * nz - 1, 1), True, nx)
    sweep(ub, ua, gx, coef, 1, (2, 3 * nz - 3), False, nx)
    sweep(ua, ub, gx, coef, nz, (nz, 1), True, nx)
    sweep(ua, ub, gx, coef, nz - 1, (2, nz + 1), False, nx)
    last(adjoint, ua, lambda a, i, b, r: gx[a, nz + i, b, r:r + 8, :])


def kappa_columns(width_class):
    table = jnp.array(WIDTH_TABLE, F32)
    table = table * table / 24.0
    hits = (width_class[..., None] == jnp.arange(CLASSES, dtype=jnp.int32)).astype(F32)
    kappa = jnp.sum(hits * table, axis=-1)
    nz, nx, nb = kappa.shape
    columns = jnp.transpose(kappa, (1, 0, 2)).reshape(nx, nz * nb)
    return jnp.pad(columns, ((0, 0), (0, BLOCK - nz * nb)))


def body(sources, cotangent, width_class):
    f, g = sources, cotangent
    nf, nz, nx, ny = f.shape
    nb = ny // BLOCK
    nc = nx // 4
    nj, ng = lax.axis_size("jet"), lax.axis_size("grp")
    assert nz == DEEP and nj % 2 == 0
    j, gi = lax.axis_index("jet"), lax.axis_index("grp")
    info = jnp.stack([j % 2, (j == 0) * 1, (j == nj - 1) * 1, (gi == 0) * 1, (gi == ng - 1) * 1, gi]).astype(jnp.int32)

    swap = [(i, i ^ 1) for i in range(nj)]
    relay = [(i, i + 2) for i in range(0, nj - 2, 2)] + [(i, i - 2) for i in range(3, nj, 2)]
    up = lambda x, axis, by=1: lax.ppermute(x, axis, [(i, i + by) for i in range(lax.axis_size(axis) - by)])
    dn = lambda x, axis, by=1: lax.ppermute(x, axis, [(i + by, i) for i in range(lax.axis_size(axis) - by)])

    pf = lax.ppermute(f, "jet", swap)
    ks = kappa_columns(width_class)
    xrows = kappa_row(nf, nz) + 8
    to_up, to_dn = call(pack_x, [(xrows, ny)] * 2, [], f, g, ks)
    low, high = up(to_up, "grp"), dn(to_dn, "grp")
    yrows = 8 * nf * nz
    ypack, ksx = call(functools.partial(pack_y, nf=nf, nz=nz, nx=nx), [(yrows, ny), (nx + 8, BLOCK)], [], low, high, ks)
    py = lax.ppermute(ypack, "jet", swap)
    pks = lax.ppermute(ksx, "jet", swap)
    pg = lax.ppermute(g, "jet", swap)
    kup, kdn = up(ksx, "jet", 2), dn(ksx, "jet", 2)
    rf = lax.ppermute(pf, "jet", relay)
    ry = lax.ppermute(py, "jet", relay)
    rks = lax.ppermute(pks, "jet", relay)
    rg = lax.ppermute(pg, "jet", relay)

    xr = nx + 32
    deep = (nf, 3 * nz, nb, xr, BLOCK)
    co = (3 * nz, nb, xr, BLOCK)
    u3, gx, cz, cx, cm, cp, inv, rc = call(
        before,
        [(nf, nz + 2, nb, xr, BLOCK), deep, (3 * nz + 1, nb, xr, BLOCK), co, co, co, co, (2 * nf * nz * nc, BLOCK)],
        [deep, deep, deep, (3 * nz + 2, nb, xr, BLOCK), (nz, nb, xr, BLOCK), (nf * nz, nb, nx, BLOCK)],
        info, f, g, pf, pg, rf, rg, low, high, py, ry, ksx, pks, rks, kdn, kup, smem=1)
    whole = lax.all_gather(rc, "grp", axis=0, tiled=True)
    nr = ng * nc
    shape = (2 * nf * nz * 16, BLOCK)
    est, mu, md = call(
        functools.partial(coarse, nf=nf, nz=nz, ng=ng, nc=nc, nb=nb),
        [shape] * 3,
        [(2 * nf * nz, nr, BLOCK), (2 * nf, nr + 16, BLOCK), (2 * nf, nr + 16, BLOCK), (nz, nr + 16, BLOCK), (5, nr, BLOCK)],
        info, whole, smem=1)
    elo, ehi = up(mu, "jet"), dn(md, "jet")
    filtered, adjoint = call(
        after, [f.shape, g.shape], [deep, deep, (xr, BLOCK)],
        info, f, u3, gx, cz, cx, cm, cp, inv, est, elo, ehi, smem=1)
    return filtered, adjoint


def solution(mesh):
    placed = (P(None, "jet", "grp", None), P(None, "jet", "grp", None), P("jet", "grp", None))
    return jax.shard_map(
        body,
        mesh=mesh,
        in_specs=placed,
        out_specs=(P(None, "jet", "grp", None), P(None, "jet", "grp", None)),
        check_vma=False,
    )
```

```python
import functools

import jax
import jax.numpy as jnp
from jax import lax
from jax.experimental import pallas as pl
from jax.experimental.pallas import tpu as pltpu
from jax.sharding import PartitionSpec as P


BLOCK = 128
CLASSES = 8
COARSE_SWEEPS = 8
DEEP = 3
O = 16
LO = 8
WIDTH_TABLE = (2.5, 3.5, 4.5, 5.0, 6.0, 7.0, 8.5, 10.0)
RELAXATION = 0.8
COARSE_RELAX = 0.8
F32 = jnp.float32
BF16 = jnp.bfloat16


VM = pl.BlockSpec(memory_space=pltpu.VMEM)
SM = pl.BlockSpec(memory_space=pltpu.SMEM)


def padded(shape):
    n = 4
    for d in shape[:-2]:
        n *= d
    return n * (-(-shape[-2] // 8) * 8) * (-(-shape[-1] // BLOCK) * BLOCK)


def call(kernel, outs, scratch, *args, smem=0, cost=(1000000, 1000000)):
    specs = [SM] * smem + [VM] * (len(args) - smem)
    need = sum(map(padded, scratch))
    return pl.pallas_call(
        kernel,
        out_shape=[jax.ShapeDtypeStruct(s, F32) for s in outs],
        in_specs=specs,
        out_specs=[VM] * len(outs),
        scratch_shapes=[pltpu.VMEM(s, F32) for s in scratch],
        cost_estimate=pl.CostEstimate(flops=cost[0], bytes_accessed=cost[1], transcendentals=0),
        compiler_params=pltpu.CompilerParams(vmem_limit_bytes=need + (6 << 20)),
    )(*args)


def iota(shape, dim):
    return lax.broadcasted_iota(jnp.int32, shape, dim)


def pack_x(info, f, g, ks, to_a, to_b):
    nf, nz, nx, ny = f.shape
    even = info[6] == 0
    kr = kappa_row(nf, nz)

    def put(at, rows, first, last):
        to_a[at:at + rows, 0:last.shape[1]] = jnp.where(even, last, first)
        to_b[at:at + rows, 0:last.shape[1]] = jnp.where(even, first, last)

    for s, ref in enumerate((f, g)):
        for a in range(nf):
            for p in range(nz):
                put(((s * nf + a) * nz + p) * DEEP, DEEP, ref[a, p, 0:DEEP, :], ref[a, p, nx - DEEP:nx, :])
    for ref in (to_a, to_b):
        ref[kr:kr + 8, :] = jnp.zeros((8, ny), F32)
    put(kr, 4, ks[0:4, :], ks[nx - 4:nx, :])


def kappa_row(nf, nz):
    return -(-2 * nf * nz * DEEP // 8) * 8


def pack_y(info, xa, xb, ks, out, low, high, *, nf, nz, nx):
    even = info[6] == 0
    low[...] = jnp.where(even, xb[...], xa[...])
    high[...] = jnp.where(even, xa[...], xb[...])
    for a in range(2 * nf):
        for p in range(nz):
            src = (a * nz + p) * DEEP
            at = (a * nz + p) * 4
            out[at:at + 2, :] = low[src + 1:src + 3, :]
            out[at + 2:at + 4, :] = high[src:src + 2, :]
    kr = kappa_row(nf, nz)
    at = 8 * nf * nz
    out[at:at + nx // 2, 0:BLOCK] = ks[0:nx // 2, :]
    out[at:at + nx // 2, BLOCK:2 * BLOCK] = ks[nx // 2:nx, :]
    out[at:at + 4, 2 * BLOCK:3 * BLOCK] = low[kr:kr + 4, 0:BLOCK]
    out[at + 4:at + 8, 2 * BLOCK:3 * BLOCK] = high[kr:kr + 4, 0:BLOCK]
    out[at + 8:at + nx // 2, 2 * BLOCK:3 * BLOCK] = jnp.zeros((nx // 2 - 8, BLOCK), F32)


def columns_of(pack, at, nx):
    half = nx // 2
    return (
        (O - 4, pack[at:at + 4, 2 * BLOCK:3 * BLOCK]),
        (O, pack[at:at + half, 0:BLOCK]),
        (O + half, pack[at:at + half, BLOCK:2 * BLOCK]),
        (O + nx, pack[at + 4:at + 8, 2 * BLOCK:3 * BLOCK]),
    )


def dot01(x, m):
    h = x.astype(BF16)
    r = x - h.astype(F32)
    i = r.astype(BF16)
    j = (r - i.astype(F32)).astype(BF16)
    dot = functools.partial(jnp.dot, preferred_element_type=F32)
    return dot(h, m) + dot(i, m) + dot(j, m)


def lane_sum(b):
    l, m = iota((BLOCK, BLOCK), 0), iota((BLOCK, BLOCK), 1)
    return jnp.where((l + b * BLOCK) // 4 == m, 1.0 / 16.0, 0.0).astype(BF16)


def lane_copy(ny):
    m, l = iota((BLOCK, ny), 0), iota((BLOCK, ny), 1)
    return jnp.where(l // 4 == m, 1.0, 0.0).astype(BF16)


def around(v, nb, lane):
    rl = [pltpu.roll(x, 1, 1) for x in v]
    rr = [pltpu.roll(x, BLOCK - 1, 1) for x in v]
    left = [jnp.where(lane == 0, rl[i - 1] if i > 0 else 0.0, rl[i]) for i in range(nb)]
    right = [jnp.where(lane == BLOCK - 1, rr[i + 1] if i < nb - 1 else 0.0, rr[i]) for i in range(nb)]
    return left, right


def pull(src, co, p, r, a, nb, lane):
    czm, czp, cxm, cxp, cym, cyp = co
    v = [src[a, p, b, r:r + 8, :] for b in range(nb)]
    left, right = around(v, nb, lane)
    out = []
    for b in range(nb):
        s = czm[b] * src[a, p - 1, b, r:r + 8, :] + czp[b] * src[a, p + 1, b, r:r + 8, :]
        s = s + cxm[b] * src[a, p, b, r - 1:r + 7, :] + cxp[b] * src[a, p, b, r + 1:r + 9, :]
        s = s + cym[b] * left[b] + cyp[b] * right[b]
        out.append(s)
    return v, out


def coefs_at(coef, p, r, nb):
    cz, cx, cm, cp, _ = coef
    return (
        [cz[p, b, r:r + 8, :] for b in range(nb)],
        [cz[p + 1, b, r:r + 8, :] for b in range(nb)],
        [cx[p, b, r - 1:r + 7, :] for b in range(nb)],
        [cx[p, b, r:r + 8, :] for b in range(nb)],
        [cm[p, b, r:r + 8, :] for b in range(nb)],
        [cp[p, b, r:r + 8, :] for b in range(nb)],
    )


def rows_of(wide, nx):
    return range(LO, LO + nx + 16, 8) if wide else range(O, O + nx, 8)


def sweep(dst, src, rhs, coef, first, count, stride, wide, nx):
    inv = coef[4]
    nf, nb = src.shape[0], src.shape[2]
    lane = iota((8, BLOCK), 1)

    def plane(i, _):
        p = first + i * stride
        for r in rows_of(wide, nx):
            co = coefs_at(coef, p, r, nb)
            w = [inv[p, b, r:r + 8, :] for b in range(nb)]
            for a in range(nf):
                v, s = pull(src, co, p, r, a, nb, lane)
                for b in range(nb):
                    dst[a, p, b, r:r + 8, :] = (1.0 - RELAXATION) * v[b] + w[b] * (rhs[a, p, b, r:r + 8, :] + s[b])
        return 0

    lax.fori_loop(0, count, plane, 0)


def three(ua, ub, rhs, coef, nz, nx):
    sweep(ub, ua, rhs, coef, 2, 2 * nz - 1, 1, True, nx)
    sweep(ub, ua, rhs, coef, 1, 2, 3 * nz - 3, False, nx)
    sweep(ua, ub, rhs, coef, nz, nz, 1, True, nx)
    sweep(ua, ub, rhs, coef, nz - 1, 2, nz + 1, False, nx)


def final(dst, src, rhs, coef, nz, nx):
    inv = coef[4]
    nf, nb = src.shape[0], src.shape[2]
    lane = iota((8, BLOCK), 1)

    def plane(i, _):
        p = nz + i
        for r in rows_of(False, nx):
            co = coefs_at(coef, p, r, nb)
            w = [inv[p, b, r:r + 8, :] for b in range(nb)]
            for a in range(nf):
                v, s = pull(src, co, p, r, a, nb, lane)
                for b in range(nb):
                    c = slice(b * BLOCK, (b + 1) * BLOCK)
                    q = r - O
                    dst[a, i, q:q + 8, c] = (1.0 - RELAXATION) * v[b] + w[b] * (rhs[a, i, q:q + 8, c] + s[b])
        return 0

    lax.fori_loop(0, nz, plane, 0)


def restrict_residual(out, base, src, rhs, coef, diag, tmp, parts, nz, nx):
    nf, nb = src.shape[0], src.shape[2]
    lane = iota((8, BLOCK), 1)

    def plane(i, _):
        p = nz + i
        for r in rows_of(False, nx):
            co = coefs_at(coef, p, r, nb)
            d = [diag[i, b, r:r + 8, :] for b in range(nb)]
            for a in range(nf):
                v, s = pull(src, co, p, r, a, nb, lane)
                for b in range(nb):
                    c = slice(b * BLOCK, (b + 1) * BLOCK)
                    q = r - O
                    tmp[b, a * nz + i, q:q + 8, :] = rhs[a, i, q:q + 8, c] - d[b] * v[b] + s[b]
        return 0

    lax.fori_loop(0, nz, plane, 0)
    nc = nx // 4
    total = None
    for b in range(nb):
        for k in range(nf * nz):
            parts[k * nc:(k + 1) * nc, :] = sum(tmp[b, k, pl.ds(j, nc, stride=4), :] for j in range(4))
        dot = dot01(parts[...], lane_sum(b))
        total = dot if total is None else total + dot
    out[base:base + total.shape[0], :] = total


def coarse_kappa(out, ks, tmp, nz, nx, nb):
    nc = nx // 4
    tmp[0, 0, 0:nx, :] = ks[...]
    kc = sum(tmp[0, 0, pl.ds(j, nc, stride=4), :] for j in range(4)) * (1.0 / 64.0)
    for p in range(nz):
        l, m = iota((BLOCK, BLOCK), 0), iota((BLOCK, BLOCK), 1)
        pick = jnp.where((l - p * nb == m - (BLOCK - nb)) & (m >= BLOCK - nb), 1.0, 0.0).astype(BF16)
        rows = slice(p * nc, (p + 1) * nc)
        out[rows, :] = out[rows, :] + dot01(kc, pick)


def coefficients(info, ka, kb, own, partner, other, cz, cx, cm, cp, inv, diag, kap, *, nz, nx, nb, at):
    first_j, last_j, first_g, last_g = (info[i] for i in range(1, 5))
    pbase = jnp.where(info[0] == 0, 1 + 2 * nz, 1)
    for base, ref in ((pbase, partner), (2 + 2 * nz - pbase, other), (1 + nz, own)):
        for row, value in columns_of(ref, at, nx):
            n = value.shape[0]
            for p in range(nz):
                for b in range(nb):
                    c = p * nb + b
                    kap[base + p, b, row:row + n, :] = jnp.broadcast_to(value[:, c:c + 1], (n, BLOCK))
    lo2 = jnp.where(info[7] == 0, kb[...], ka[...])
    hi2 = jnp.where(info[7] == 0, ka[...], kb[...])
    for b in range(nb):
        c = (nz - 1) * nb + b
        kap[0, b, O:O + nx, :] = jnp.broadcast_to(lo2[:, c:c + 1], (nx, BLOCK))
        kap[3 * nz + 1, b, O:O + nx, :] = jnp.broadcast_to(hi2[:, b:b + 1], (nx, BLOCK))
    lane = iota((8, BLOCK), 1)

    def cplane(p, _):
        out = ((first_j == 1) & (p < nz)) | ((last_j == 1) & (p >= 2 * nz))
        for r in rows_of(True, nx):
            row = iota((8, BLOCK), 0) + (r - O)
            here = jnp.where(((row < 0) & (first_g == 1)) | ((row >= nx) & (last_g == 1)) | out, 0.0, RELAXATION)
            s8 = slice(r, r + 8)
            k = [kap[p + 1, b, s8, :] for b in range(nb)]
            for b in range(nb):
                zm = 0.5 * (kap[p, b, s8, :] + k[b])
                zp = 0.5 * (k[b] + kap[p + 2, b, s8, :])
                xp = 0.5 * (k[b] + kap[p + 1, b, r + 1:r + 9, :])
                xm = 0.5 * (k[b] + kap[p + 1, b, r - 1:r + 7, :])
                ym = jnp.where(lane == 0, 0.5 * (k[b] + k[b - 1]) if b > 0 else 0.5 * k[b], k[b])
                yp = jnp.where(lane == BLOCK - 1, 0.5 * (k[b] + k[b + 1]) if b < nb - 1 else 0.5 * k[b], k[b])
                cz[p, b, s8, :] = zm
                cz[p + 1, b, s8, :] = zp
                cx[p, b, s8, :] = xp
                cm[p, b, s8, :] = ym
                cp[p, b, s8, :] = yp
                d = 1.0 + zm + zp + xm + xp + ym + yp
                inv[p, b, s8, :] = here / d

                @pl.when((p >= nz) & (p < 2 * nz))
                def _():
                    diag[p - nz, b, s8, :] = d
        return 0

    lax.fori_loop(0, 3 * nz, cplane, 0)


def lay(dst, ref, a, p, q, rows, lo_row, hi_row, nx, nb):
    width, _, pack = rows
    for b in range(nb):
        c = slice(b * BLOCK, (b + 1) * BLOCK)
        dst[a, q, b, O:O + nx, :] = ref[a, p, :, c]
        if pack is not None:
            dst[a, q, b, O - width:O, :] = pack[0][lo_row:lo_row + width, c]
            dst[a, q, b, O + nx:O + nx + width, :] = pack[1][hi_row:hi_row + width, c]


def ends(low, high, s, a, p, nf, nz):
    at = ((s * nf + a) * nz + p) * DEEP
    return (DEEP, None, (low, high)), at, at


def corners(pack, s, a, p, nf, nz):
    at = ((s * nf + a) * nz + p) * 4
    return (2, None, (pack, pack)), at, at + 2


def start(dst, own, inv, p, nx, nb, nf):
    for a in range(nf):
        for b in range(nb):
            for r in rows_of(True, nx):
                dst[a, p, b, r:r + 8, :] = inv[p, b, r:r + 8, :] * own[a, p, b, r:r + 8, :]


def fwd_before(info, f, pf, rf, low, high, py, ry, ks, cz, cx, cm, cp, inv, diag, u3, rc, fx, ub, tmp, parts):
    nf, nz, nx, ny = f.shape
    nb = ny // BLOCK
    par = info[0]
    pbase = jnp.where(par == 0, 2 * nz, 0)
    rbase = 2 * nz - pbase
    for a in range(nf):
        for p in range(nz):
            lay(fx, f, a, p, nz + p, *ends(low, high, 0, a, p, nf, nz), nx, nb)
            lay(fx, pf, a, p, pbase + p, *corners(py, 0, a, p, nf, nz), nx, nb)
            lay(fx, rf, a, p, rbase + p, *corners(ry, 0, a, p, nf, nz), nx, nb)
    coef = (cz, cx, cm, cp, inv)

    def one(p, _):
        start(u3, fx, inv, p, nx, nb, nf)
        return 0

    lax.fori_loop(0, 3 * nz, one, 0)
    three(u3, ub, fx, coef, nz, nx)
    restrict_residual(rc, 0, u3, f, coef, diag, tmp, parts, nz, nx)
    coarse_kappa(rc, ks, tmp, nz, nx, nb)


def adj_before(info, g, pg, rn, low, high, rcf, cz, cx, cm, cp, inv, diag, rc, gx, ua, tmp, parts):
    nf, nz, nx, ny = g.shape
    nb = ny // BLOCK
    par = info[0]
    pp = jnp.where(par == 0, 2 * nz, nz - 1)
    rp = 3 * nz - 1 - pp
    near = jnp.where(par == 0, 0, nz - 1)
    none = (0, None, None)
    for a in range(nf):
        for p in range(nz):
            lay(gx, g, a, p, nz + p, *ends(low, high, 1, a, p, nf, nz), nx, nb)
        lay(gx, pg, a, near, pp, none, 0, 0, nx, nb)
        lay(gx, rn, a, 0, rp, none, 0, 0, nx, nb)

    def one(p, _):
        start(ua, gx, inv, p, nx, nb, nf)
        return 0

    lax.fori_loop(nz - 1, 2 * nz + 1, one, 0)
    n = rcf.shape[0]
    rc[0:n, :] = rcf[...]
    restrict_residual(rc, n, ua, g, (cz, cx, cm, cp, inv), diag, tmp, parts, nz, nx)


def prolong(dst, e, k, a, q, nx, nb):
    nc = nx // 4
    for b in range(nb):
        part = e[k * 16:k * 16 + nc + 2, b * BLOCK:(b + 1) * BLOCK]
        for j in range(4):
            dst[a, q, b, pl.ds(O - 4 + j, nc + 2, stride=4), :] = part


def fwd_after(info, f, u3, cz, cx, cm, cp, inv, est, ea, eb, filtered, ua, e):
    nf, nz, nx, ny = f.shape
    nb = ny // BLOCK
    copy = lane_copy(ny)
    coef = (cz, cx, cm, cp, inv)
    qa = jnp.where(info[0] == 0, 2 * nz, nz - 1)
    for ref, slots, base in ((est, nz, nz), (ea, 1, qa), (eb, 1, 3 * nz - 1 - qa)):
        n = nf * slots * 16
        e[0:n, :] = dot01(ref[0:n, :], copy)
        for a in range(nf):
            for i in range(slots):
                prolong(ua, e, a * slots + i, a, base + i, nx, nb)

    def one(p, _):
        for a in range(nf):
            for b in range(nb):
                for r in rows_of(True, nx):
                    ua[a, p, b, r:r + 8, :] = ua[a, p, b, r:r + 8, :] + u3[a, p, b, r:r + 8, :]
        return 0

    lax.fori_loop(nz - 1, 2 * nz + 1, one, 0)
    final(filtered, ua, f, coef, nz, nx)


def adj_after(info, g, pg, rn, rr, low, high, py, ry, cz, cx, cm, cp, inv, est, ea, eb, adjoint, gx, ua, ub, e):
    nf, nz, nx, ny = g.shape
    nb = ny // BLOCK
    par = info[0]
    pbase = jnp.where(par == 0, 2 * nz, 0)
    rbase = 2 * nz - pbase
    near = jnp.where(par == 0, nz - 1, 0)
    rest = jnp.where(par == 0, 0, 1)
    for a in range(nf):
        for p in range(nz):
            lay(gx, g, a, p, nz + p, *ends(low, high, 1, a, p, nf, nz), nx, nb)
            lay(gx, pg, a, p, pbase + p, *corners(py, 1, a, p, nf, nz), nx, nb)
        lay(gx, rn, a, 0, rbase + near, (0, None, None), 0, 0, nx, nb)
        for p in range(nz - 1):
            lay(gx, rr, a, p, rbase + rest + p, (0, None, None), 0, 0, nx, nb)
        for p in range(nz):
            (width, _, pack), lo_row, hi_row = corners(ry, 1, a, p, nf, nz)
            for b in range(nb):
                c = slice(b * BLOCK, (b + 1) * BLOCK)
                gx[a, rbase + p, b, O - width:O, :] = ry[lo_row:lo_row + width, c]
                gx[a, rbase + p, b, O + nx:O + nx + width, :] = ry[hi_row:hi_row + width, c]
    copy = lane_copy(ny)
    coef = (cz, cx, cm, cp, inv)
    n = nf * nz * 16
    for ref, at, base in ((est, n, nz), (ea, nf * 16, pbase), (eb, nf * 16, rbase)):
        e[...] = dot01(ref[at:at + n, :], copy)
        for a in range(nf):
            for i in range(nz):
                prolong(ua, e, a * nz + i, a, base + i, nx, nb)

    def one(p, _):
        for b in range(nb):
            for r in rows_of(True, nx):
                w = inv[p, b, r:r + 8, :]
                for a in range(nf):
                    ua[a, p, b, r:r + 8, :] = ua[a, p, b, r:r + 8, :] + w * gx[a, p, b, r:r + 8, :]
        return 0

    lax.fori_loop(0, 3 * nz, one, 0)
    three(ua, ub, gx, coef, nz, nx)
    final(adjoint, ua, g, coef, nz, nx)


def coarse(info, rc, est, to_a, to_b, full, e0, e1, ck, cf, *, nf, nz, ng, nc, nb):
    half = nf
    nf = 2 * nf
    nr = ng * nc
    per = rc.shape[0] // ng
    lane = iota((8, BLOCK), 1)
    used = BLOCK // 4 * nb
    valid = lane < used
    zero = jnp.zeros((8, BLOCK), F32)
    for ref in (e0, e1, ck):
        for a in range(ref.shape[0]):
            ref[a, 0:8, :] = zero
            ref[a, 8 + nr:16 + nr, :] = zero
    at = info[5] * nc
    for k in range(nf * nz):
        for i in range(ng):
            row = i * per + (0 if k < half * nz else per // 2) + (k % (half * nz)) * nc
            full[k, i * nc:(i + 1) * nc, :] = rc[row:row + nc, :]
    for p in range(nz):
        for r in range(0, nr, 8):
            raw = full[p, r:r + 8, :]
            kc = zero
            for b in range(nb):
                column = jnp.broadcast_to(raw[:, BLOCK - nb + b:BLOCK - nb + b + 1], (8, BLOCK))
                kc = jnp.where(lane // (BLOCK // 4) == b, column, kc)
            ck[p, 8 + r:16 + r, :] = kc
            full[p, r:r + 8, :] = jnp.where(valid, raw, 0.0)
    for p in range(nz):
        dsum = zero
        rsum = [zero] * nf
        for r in range(0, nr, 8):
            s8 = slice(r, r + 8)
            k = ck[p, 8 + r:16 + r, :]
            xm = jnp.where(valid, 0.5 * (k + ck[p, 7 + r:15 + r, :]), 0.0)
            xp = jnp.where(valid, 0.5 * (k + ck[p, 9 + r:17 + r, :]), 0.0)
            ym = jnp.where(valid, 0.5 * (k + pltpu.roll(k, 1, 1)), 0.0)
            yp = jnp.where(valid, 0.5 * (k + pltpu.roll(k, BLOCK - 1, 1)), 0.0)
            d = 1.0 + xm + xp + ym + yp
            dsum = dsum + jnp.where(valid, d, 0.0)
            ci = jnp.where(valid, COARSE_RELAX / d, 0.0)
            cf[0, s8, :] = xm
            cf[1, s8, :] = xp
            cf[2, s8, :] = ym
            cf[3, s8, :] = yp
            cf[4, s8, :] = ci
            for a in range(nf):
                v = full[a * nz + p, s8, :]
                rsum[a] = rsum[a] + v
                e0[a, 8 + r:16 + r, :] = ci * v
        total = jnp.sum(dsum)
        shift = [jnp.sum(rsum[a]) / total for a in range(nf)]
        src, dst = e0, e1
        for n in range(COARSE_SWEEPS - 1):
            for r in range(0, nr, 8):
                s8 = slice(r, r + 8)
                c = [cf[i, s8, :] for i in range(5)]
                for a in range(nf):
                    v = src[a, 8 + r:16 + r, :]
                    s = c[0] * src[a, 7 + r:15 + r, :] + c[1] * src[a, 9 + r:17 + r, :]
                    s = s + c[2] * pltpu.roll(v, 1, 1) + c[3] * pltpu.roll(v, BLOCK - 1, 1)
                    v = (1.0 - COARSE_RELAX) * v + c[4] * (full[a * nz + p, s8, :] + s)
                    if n == COARSE_SWEEPS - 2:
                        v = jnp.where(valid, v + shift[a], 0.0)
                    dst[a, 8 + r:16 + r, :] = v
            src, dst = dst, src
        for a in range(nf):
            own = src[a, pl.ds(at + 7, 16), :]
            k = a * nz + p
            est[k * 16:(k + 1) * 16, :] = own
            if a >= half:
                m = (half + k - half * nz) * 16
                to_a[m:m + 16, :] = own
                to_b[m:m + 16, :] = own
            elif p in (0, nz - 1):
                m = slice(a * 16, (a + 1) * 16)

                @pl.when((info[0] == 0) == (p == nz - 1))
                def _():
                    to_a[m, :] = own

                @pl.when((info[0] == 0) == (p == 0))
                def _():
                    to_b[m, :] = own


def kappa_columns(width_class):
    table = jnp.array(WIDTH_TABLE, F32)
    table = table * table / 24.0
    hits = (width_class[..., None] == jnp.arange(CLASSES, dtype=jnp.int32)).astype(F32)
    kappa = jnp.sum(hits * table, axis=-1)
    nz, nx, nb = kappa.shape
    columns = jnp.transpose(kappa, (1, 0, 2)).reshape(nx, nz * nb)
    return jnp.pad(columns, ((0, 0), (0, BLOCK - nz * nb)))


def cycle(f, g, width_class):
    nf, nz, nx, ny = f.shape
    nb = ny // BLOCK
    nc = nx // 4
    nj, ng = lax.axis_size("jet"), lax.axis_size("grp")
    assert nz == DEEP and nj % 2 == 0
    j, gi = lax.axis_index("jet"), lax.axis_index("grp")
    par = j % 2
    zp = (j // 2) % 2
    info = jnp.stack([par, (j == 0) * 1, (j == nj - 1) * 1, (gi == 0) * 1, (gi == ng - 1) * 1, gi, gi % 2, zp]).astype(jnp.int32)

    def both(pairs):
        return [p for a, b in pairs for p in ((a, b), (b, a))]

    swap = both([(i, i + 1) for i in range(0, nj, 2)])
    side = both([(i, i + 1) for i in range(1, nj - 1, 2)])
    relay = [(i, i + 2) for i in range(0, nj - 2, 2)] + [(i, i - 2) for i in range(3, nj, 2)]
    two_a = both([(i, i + 2) for i in range(nj - 2) if (i // 2) % 2 == 0])
    two_b = both([(i, i + 2) for i in range(nj - 2) if (i // 2) % 2 == 1])
    x_a = both([(i, i + 1) for i in range(0, ng - 1, 2)])
    x_b = both([(i, i + 1) for i in range(1, ng - 1, 2)])

    pf = lax.ppermute(f, "jet", swap)
    ks = kappa_columns(width_class)
    ka, kb = lax.ppermute(ks, "jet", two_a), lax.ppermute(ks, "jet", two_b)
    xs = (kappa_row(nf, nz) + 8, ny)
    to_a, to_b = call(pack_x, [xs] * 2, [], info, f, g, ks, smem=1)
    xa, xb = lax.ppermute(to_a, "grp", x_a), lax.ppermute(to_b, "grp", x_b)
    krow = 8 * nf * nz
    ypack, low, high = call(functools.partial(pack_y, nf=nf, nz=nz, nx=nx), [(krow + nx // 2, ny), xs, xs], [], info, xa, xb, ks, smem=1)
    py = lax.ppermute(ypack, "jet", swap)
    ry = lax.ppermute(ypack, "jet", side)
    pg = lax.ppermute(g, "jet", swap)
    rf = lax.ppermute(pf, "jet", relay)
    near = lax.dynamic_slice_in_dim(pg, (1 - par) * (nz - 1), 1, 1)
    rest = lax.dynamic_slice_in_dim(pg, par, nz - 1, 1)
    rn = lax.ppermute(near, "jet", relay)
    rr = lax.ppermute(rest, "jet", relay)

    xr = nx + 32
    deep = (nf, 3 * nz, nb, xr, BLOCK)
    co = (3 * nz, nb, xr, BLOCK)
    coefs = call(
        functools.partial(coefficients, nz=nz, nx=nx, nb=nb, at=krow),
        [(3 * nz + 1, nb, xr, BLOCK), co, co, co, co, (nz, nb, xr, BLOCK)], [(3 * nz + 2, nb, xr, BLOCK)],
        info, ka, kb, ypack, py, ry, smem=1)
    coef, diag = coefs[:5], coefs[5]
    rows = -(-nf * nz * nc // 8) * 8
    scratch = [(nb, nf * nz, nx, BLOCK), (rows, BLOCK)]
    u3, rcf = call(fwd_before, [deep, (rows, BLOCK)], [deep, deep] + scratch, info, f, pf, rf, low, high, py, ry, ks, *coef, diag, smem=1)
    (rc,) = call(adj_before, [(2 * rows, BLOCK)], [deep, deep] + scratch, info, g, pg, rn, low, high, rcf, *coef, diag, smem=1)
    whole = lax.all_gather(rc, "grp", axis=0, tiled=True)
    nr = ng * nc
    solve = [(2 * nf * nz, nr, BLOCK), (2 * nf, nr + 16, BLOCK), (2 * nf, nr + 16, BLOCK), (nz, nr + 16, BLOCK), (5, nr, BLOCK)]
    sent = (nf * (nz + 1) * 16, BLOCK)
    est, to_a, to_b = call(
        functools.partial(coarse, nf=nf, nz=nz, ng=ng, nc=nc, nb=nb),
        [(2 * nf * nz * 16, BLOCK), sent, sent], solve, info, whole, smem=1)
    ea, eb = lax.ppermute(to_a, "jet", swap), lax.ppermute(to_b, "jet", side)
    (filtered,) = call(fwd_after, [f.shape], [deep, (nf * nz * 16, ny)], info, f, u3, *coef, est, ea, eb, smem=1)
    (adjoint,) = call(adj_after, [g.shape], [deep, deep, deep, (nf * nz * 16, ny)], info, g, pg, rn, rr, low, high, py, ry, *coef, est, ea, eb, smem=1)
    return filtered, adjoint


def solution(mesh):
    placed = (P(None, "jet", "grp", None), P(None, "jet", "grp", None), P("jet", "grp", None))
    return jax.shard_map(
        cycle,
        mesh=mesh,
        in_specs=placed,
        out_specs=(P(None, "jet", "grp", None), P(None, "jet", "grp", None)),
        check_vma=False,
    )
```

```python
import functools

import jax
import jax.numpy as jnp
from jax import lax
from jax.experimental import pallas as pl
from jax.experimental.pallas import tpu as pltpu
from jax.sharding import PartitionSpec as P


BLOCK = 128
CLASSES = 8
COARSE_SWEEPS = 8
DEEP = 3
O = 16
LO = 8
WIDTH_TABLE = (2.5, 3.5, 4.5, 5.0, 6.0, 7.0, 8.5, 10.0)
RELAXATION = 0.8
COARSE_RELAX = 0.8
F32 = jnp.float32
BF16 = jnp.bfloat16


VM = pl.BlockSpec(memory_space=pltpu.VMEM)
SM = pl.BlockSpec(memory_space=pltpu.SMEM)


def padded(shape):
    n = 4
    for d in shape[:-2]:
        n *= d
    return n * (-(-shape[-2] // 8) * 8) * (-(-shape[-1] // BLOCK) * BLOCK)


def call(kernel, outs, scratch, *args, smem=0, alias=None, cost=(1000000, 1000000)):
    specs = [SM] * smem + [VM] * (len(args) - smem)
    need = sum(map(padded, scratch))
    return pl.pallas_call(
        kernel,
        out_shape=[jax.ShapeDtypeStruct(s, F32) for s in outs],
        in_specs=specs,
        out_specs=[VM] * len(outs),
        scratch_shapes=[pltpu.VMEM(s, F32) for s in scratch],
        input_output_aliases=alias or {},
        cost_estimate=pl.CostEstimate(flops=cost[0], bytes_accessed=cost[1], transcendentals=0),
        compiler_params=pltpu.CompilerParams(vmem_limit_bytes=need + (6 << 20)),
    )(*args)


def iota(shape, dim):
    return lax.broadcasted_iota(jnp.int32, shape, dim)


def pack_x(info, f, g, to_a, to_b):
    nf, nz, nx, _ = f.shape
    even = info[6] == 0
    for s, ref in enumerate((f, g)):
        for a in range(nf):
            for p in range(nz):
                at = ((s * nf + a) * nz + p) * DEEP
                first, last = ref[a, p, 0:DEEP, :], ref[a, p, nx - DEEP:nx, :]
                to_a[at:at + DEEP, :] = jnp.where(even, last, first)
                to_b[at:at + DEEP, :] = jnp.where(even, first, last)


def pack_k(info, a_in, b_in, ks, kp, ko, ka, kb, to_a, to_b, cols, *, nf, nz, nb):
    nx = ks.shape[0]
    n = nz * nb
    lane = iota((nx, BLOCK), 1)

    def shift(x, at):
        return x if at % BLOCK == 0 else pltpu.roll(x, at % BLOCK, 1)

    def only(x, first, count, outside=None):
        keep = (lane >= first) & (lane < first + count)
        if outside is not None:
            keep = keep & (outside == 0)
        return jnp.where(keep, x, 0.0)

    up, far = info[0] == 0, info[7] == 0
    lo1, hi1 = jnp.where(up, ko[...], kp[...]), jnp.where(up, kp[...], ko[...])
    lo2, hi2 = jnp.where(far, kb[...], ka[...]), jnp.where(far, ka[...], kb[...])
    kall = shift(only(lo2, n - nb, nb, info[8]), nb - n) + shift(only(lo1, 0, n, info[1]), nb) + shift(only(ks[...], 0, n), nb + n)
    kall = kall + shift(only(hi1, 0, n, info[2]), nb + 2 * n) + shift(only(hi2, 0, nb, info[9]), nb + 3 * n)
    cols[...] = kall
    even = info[6] == 0
    kr = kappa_row(nf, nz)
    first, last = kall[0:4, :], kall[nx - 4:nx, :]
    to_a[kr:kr + 4, 0:BLOCK] = jnp.where(even, last, first)
    to_b[kr:kr + 4, 0:BLOCK] = jnp.where(even, first, last)


def kappa_row(nf, nz):
    return -(-2 * nf * nz * DEEP // 8) * 8


def pack_y(info, xa, xb, out, low, high, *, nf, nz):
    even = info[6] == 0
    low[...] = jnp.where(even, xb[...], xa[...])
    high[...] = jnp.where(even, xa[...], xb[...])
    for a in range(2 * nf):
        for p in range(nz):
            src = (a * nz + p) * DEEP
            at = (a * nz + p) * 4
            out[at:at + 2, :] = low[src + 1:src + 3, :]
            out[at + 2:at + 4, :] = high[src:src + 2, :]


def dot01(x, m):
    h = x.astype(BF16)
    r = x - h.astype(F32)
    i = r.astype(BF16)
    j = (r - i.astype(F32)).astype(BF16)
    dot = functools.partial(jnp.dot, preferred_element_type=F32)
    return dot(h, m) + dot(i, m) + dot(j, m)


def lane_sum(b):
    l, m = iota((BLOCK, BLOCK), 0), iota((BLOCK, BLOCK), 1)
    return jnp.where((l + b * BLOCK) // 4 == m, 1.0 / 16.0, 0.0).astype(BF16)


def lane_copy(ny):
    m, l = iota((BLOCK, ny), 0), iota((BLOCK, ny), 1)
    return jnp.where(l // 4 == m, 1.0, 0.0).astype(BF16)


def around(v, nb, lane):
    rl = [pltpu.roll(x, 1, 1) for x in v]
    rr = [pltpu.roll(x, BLOCK - 1, 1) for x in v]
    left = [jnp.where(lane == 0, rl[i - 1] if i > 0 else 0.0, rl[i]) for i in range(nb)]
    right = [jnp.where(lane == BLOCK - 1, rr[i + 1] if i < nb - 1 else 0.0, rr[i]) for i in range(nb)]
    return left, right


def pull(src, co, p, r, a, nb, lane):
    czm, czp, cxm, cxp, cym, cyp = co
    v = [src[a, p, b, r:r + 8, :] for b in range(nb)]
    left, right = around(v, nb, lane)
    out = []
    for b in range(nb):
        s = czm[b] * src[a, p - 1, b, r:r + 8, :] + czp[b] * src[a, p + 1, b, r:r + 8, :]
        s = s + cxm[b] * src[a, p, b, r - 1:r + 7, :] + cxp[b] * src[a, p, b, r + 1:r + 9, :]
        s = s + cym[b] * left[b] + cyp[b] * right[b]
        out.append(s)
    return v, out


def coefs_at(coef, p, r, nb):
    cz, cx, cm, cp, _ = coef
    return (
        [cz[p, b, r:r + 8, :] for b in range(nb)],
        [cz[p + 1, b, r:r + 8, :] for b in range(nb)],
        [cx[p, b, r - 1:r + 7, :] for b in range(nb)],
        [cx[p, b, r:r + 8, :] for b in range(nb)],
        [cm[p, b, r:r + 8, :] for b in range(nb)],
        [cp[p, b, r:r + 8, :] for b in range(nb)],
    )


def rows_of(wide, nx):
    return range(LO, LO + nx + 16, 8) if wide else range(O, O + nx, 8)


def sweep(dst, src, rhs, coef, first, count, stride, wide, nx):
    inv = coef[4]
    nf, nb = src.shape[0], src.shape[2]
    lane = iota((8, BLOCK), 1)

    def plane(i, _):
        p = first + i * stride
        for r in rows_of(wide, nx):
            co = coefs_at(coef, p, r, nb)
            w = [inv[p, b, r:r + 8, :] for b in range(nb)]
            for a in range(nf):
                v, s = pull(src, co, p, r, a, nb, lane)
                for b in range(nb):
                    dst[a, p, b, r:r + 8, :] = (1.0 - RELAXATION) * v[b] + w[b] * (rhs[a, p, b, r:r + 8, :] + s[b])
        return 0

    lax.fori_loop(0, count, plane, 0)


def three(ua, ub, rhs, coef, nz, nx):
    sweep(ub, ua, rhs, coef, 2, 2 * nz - 1, 1, True, nx)
    sweep(ub, ua, rhs, coef, 1, 2, 3 * nz - 3, False, nx)
    sweep(ua, ub, rhs, coef, nz, nz, 1, True, nx)
    sweep(ua, ub, rhs, coef, nz - 1, 2, nz + 1, False, nx)


def final(dst, src, rhs, coef, nz, nx):
    inv = coef[4]
    nf, nb = src.shape[0], src.shape[2]
    lane = iota((8, BLOCK), 1)

    def plane(i, _):
        p = nz + i
        for r in rows_of(False, nx):
            co = coefs_at(coef, p, r, nb)
            w = [inv[p, b, r:r + 8, :] for b in range(nb)]
            for a in range(nf):
                v, s = pull(src, co, p, r, a, nb, lane)
                for b in range(nb):
                    c = slice(b * BLOCK, (b + 1) * BLOCK)
                    q = r - O
                    dst[a, i, q:q + 8, c] = (1.0 - RELAXATION) * v[b] + w[b] * (rhs[a, i, q:q + 8, c] + s[b])
        return 0

    lax.fori_loop(0, nz, plane, 0)


def restrict_residual(out, base, src, rhs, coef, diag, tmp, parts, nz, nx):
    nf, nb = src.shape[0], src.shape[2]
    lane = iota((8, BLOCK), 1)

    def plane(i, _):
        p = nz + i
        for r in rows_of(False, nx):
            co = coefs_at(coef, p, r, nb)
            d = [diag[i, b, r:r + 8, :] for b in range(nb)]
            for a in range(nf):
                v, s = pull(src, co, p, r, a, nb, lane)
                for b in range(nb):
                    c = slice(b * BLOCK, (b + 1) * BLOCK)
                    q = r - O
                    tmp[b, a * nz + i, q:q + 8, :] = rhs[a, i, q:q + 8, c] - d[b] * v[b] + s[b]
        return 0

    lax.fori_loop(0, nz, plane, 0)
    nc = nx // 4
    total = None
    for b in range(nb):
        for k in range(nf * nz):
            parts[k * nc:(k + 1) * nc, :] = sum(tmp[b, k, pl.ds(j, nc, stride=4), :] for j in range(4))
        dot = dot01(parts[...], lane_sum(b))
        total = dot if total is None else total + dot
    out[base:base + total.shape[0], :] = total


def coarse_kappa(out, ks, tmp, nz, nx, nb):
    nc = nx // 4
    tmp[0, 0, 0:nx, :] = ks[...]
    kc = sum(tmp[0, 0, pl.ds(j, nc, stride=4), :] for j in range(4)) * (1.0 / 64.0)
    for p in range(nz):
        l, m = iota((BLOCK, BLOCK), 0), iota((BLOCK, BLOCK), 1)
        pick = jnp.where((l - p * nb == m - (BLOCK - nb)) & (m >= BLOCK - nb), 1.0, 0.0).astype(BF16)
        rows = slice(p * nc, (p + 1) * nc)
        out[rows, :] = out[rows, :] + dot01(kc, pick)


def coefficients(info, cols, low, high, cz, cx, cm, cp, inv, diag, kap, *, nz, nx, nb, at):
    first_j, last_j, first_g, last_g = (info[i] for i in range(1, 5))
    below = jnp.where(first_g == 1, 0.0, low[at:at + 4, 0:BLOCK])
    above = jnp.where(last_g == 1, 0.0, high[at:at + 4, 0:BLOCK])
    for row, value in ((O - 4, below), (O, cols[...]), (O + nx, above)):
        n = value.shape[0]
        for p in range(3 * nz + 2):
            for b in range(nb):
                c = p * nb + b
                kap[p, b, row:row + n, :] = jnp.broadcast_to(value[:, c:c + 1], (n, BLOCK))
    lane = iota((8, BLOCK), 1)

    def cplane(p, _):
        out = ((first_j == 1) & (p < nz)) | ((last_j == 1) & (p >= 2 * nz))
        for r in rows_of(True, nx):
            row = iota((8, BLOCK), 0) + (r - O)
            here = jnp.where(((row < 0) & (first_g == 1)) | ((row >= nx) & (last_g == 1)) | out, 0.0, RELAXATION)
            s8 = slice(r, r + 8)
            k = [kap[p + 1, b, s8, :] for b in range(nb)]
            for b in range(nb):
                zm = 0.5 * (kap[p, b, s8, :] + k[b])
                zp = 0.5 * (k[b] + kap[p + 2, b, s8, :])
                xp = 0.5 * (k[b] + kap[p + 1, b, r + 1:r + 9, :])
                xm = 0.5 * (k[b] + kap[p + 1, b, r - 1:r + 7, :])
                ym = jnp.where(lane == 0, 0.5 * (k[b] + k[b - 1]) if b > 0 else 0.5 * k[b], k[b])
                yp = jnp.where(lane == BLOCK - 1, 0.5 * (k[b] + k[b + 1]) if b < nb - 1 else 0.5 * k[b], k[b])
                cz[p, b, s8, :] = zm
                cz[p + 1, b, s8, :] = zp
                cx[p, b, s8, :] = xp
                cm[p, b, s8, :] = ym
                cp[p, b, s8, :] = yp
                d = 1.0 + zm + zp + xm + xp + ym + yp
                inv[p, b, s8, :] = here / d

                @pl.when((p >= nz) & (p < 2 * nz))
                def _():
                    diag[p - nz, b, s8, :] = d
        return 0

    lax.fori_loop(0, 3 * nz, cplane, 0)


def lay(dst, ref, a, p, q, rows, lo_row, hi_row, nx, nb):
    width, _, pack = rows
    for b in range(nb):
        c = slice(b * BLOCK, (b + 1) * BLOCK)
        dst[a, q, b, O:O + nx, :] = ref[a, p, :, c]
        if pack is not None:
            dst[a, q, b, O - width:O, :] = pack[0][lo_row:lo_row + width, c]
            dst[a, q, b, O + nx:O + nx + width, :] = pack[1][hi_row:hi_row + width, c]


def ends(low, high, s, a, p, nf, nz):
    at = ((s * nf + a) * nz + p) * DEEP
    return (DEEP, None, (low, high)), at, at


def corners(pack, s, a, p, nf, nz):
    at = ((s * nf + a) * nz + p) * 4
    return (2, None, (pack, pack)), at, at + 2


def start(dst, own, inv, p, nx, nb, nf):
    for a in range(nf):
        for b in range(nb):
            for r in rows_of(True, nx):
                dst[a, p, b, r:r + 8, :] = inv[p, b, r:r + 8, :] * own[a, p, b, r:r + 8, :]


def fwd_before(info, f, pf, rf, low, high, py, ry, ks, cz, cx, cm, cp, inv, diag, u3, rc, fx, ub, tmp, parts):
    nf, nz, nx, ny = f.shape
    nb = ny // BLOCK
    par = info[0]
    pbase = jnp.where(par == 0, 2 * nz, 0)
    rbase = 2 * nz - pbase
    for a in range(nf):
        for p in range(nz):
            lay(fx, f, a, p, nz + p, *ends(low, high, 0, a, p, nf, nz), nx, nb)
            lay(fx, pf, a, p, pbase + p, *corners(py, 0, a, p, nf, nz), nx, nb)
            lay(fx, rf, a, p, rbase + p, *corners(ry, 0, a, p, nf, nz), nx, nb)
    coef = (cz, cx, cm, cp, inv)

    def one(p, _):
        start(u3, fx, inv, p, nx, nb, nf)
        return 0

    lax.fori_loop(0, 3 * nz, one, 0)
    three(u3, ub, fx, coef, nz, nx)
    restrict_residual(rc, 0, u3, f, coef, diag, tmp, parts, nz, nx)
    coarse_kappa(rc, ks, tmp, nz, nx, nb)


def adj_before(info, g, pg, rn, low, high, rcf, cz, cx, cm, cp, inv, diag, rc, gx, ua, tmp, parts):
    nf, nz, nx, ny = g.shape
    nb = ny // BLOCK
    par = info[0]
    pp = jnp.where(par == 0, 2 * nz, nz - 1)
    rp = 3 * nz - 1 - pp
    near = jnp.where(par == 0, 0, nz - 1)
    none = (0, None, None)
    for a in range(nf):
        for p in range(nz):
            lay(gx, g, a, p, nz + p, *ends(low, high, 1, a, p, nf, nz), nx, nb)
        lay(gx, pg, a, near, pp, none, 0, 0, nx, nb)
        lay(gx, rn, a, 0, rp, none, 0, 0, nx, nb)

    def one(p, _):
        start(ua, gx, inv, p, nx, nb, nf)
        return 0

    lax.fori_loop(nz - 1, 2 * nz + 1, one, 0)
    n = rcf.shape[0]
    rc[0:n, :] = rcf[...]
    restrict_residual(rc, n, ua, g, (cz, cx, cm, cp, inv), diag, tmp, parts, nz, nx)


def prolong(dst, e, k, a, q, nx, nb):
    nc = nx // 4
    for b in range(nb):
        part = e[k * 16:k * 16 + nc + 2, b * BLOCK:(b + 1) * BLOCK]
        for j in range(4):
            dst[a, q, b, pl.ds(O - 4 + j, nc + 2, stride=4), :] = part


def middle(info, u3, g, pg, rn, rr, low, high, py, ry, inv, est, uf, gx, ug, tmp, e):
    nf, nz, nx, ny = g.shape
    nb = ny // BLOCK
    par = info[0]
    pbase = jnp.where(par == 0, 2 * nz, 0)
    rbase = 2 * nz - pbase
    near = jnp.where(par == 0, nz - 1, 0)
    rest = jnp.where(par == 0, 0, 1)
    for a in range(nf):
        for p in range(nz):
            lay(gx, g, a, p, nz + p, *ends(low, high, 1, a, p, nf, nz), nx, nb)
            lay(gx, pg, a, p, pbase + p, *corners(py, 1, a, p, nf, nz), nx, nb)
        lay(gx, rn, a, 0, rbase + near, (0, None, None), 0, 0, nx, nb)
        for p in range(nz - 1):
            lay(gx, rr, a, p, rbase + rest + p, (0, None, None), 0, 0, nx, nb)
        for p in range(nz):
            (width, _, pack), lo_row, hi_row = corners(ry, 1, a, p, nf, nz)
            for b in range(nb):
                c = slice(b * BLOCK, (b + 1) * BLOCK)
                gx[a, rbase + p, b, O - width:O, :] = ry[lo_row:lo_row + width, c]
                gx[a, rbase + p, b, O + nx:O + nx + width, :] = ry[hi_row:hi_row + width, c]

    def one(p, _):
        start(ug, gx, inv, p, nx, nb, nf)
        return 0

    lax.fori_loop(0, 3 * nz, one, 0)
    e[...] = dot01(est[...], lane_copy(ny))
    for s, dst in enumerate((uf, ug)):
        for a in range(nf):
            for i in range(nz):
                prolong(tmp, e, (s * nf + a) * nz + i, a, i, nx, nb)

        def add(i, _):
            for a in range(nf):
                for b in range(nb):
                    for r in rows_of(True, nx):
                        dst[a, nz + i, b, r:r + 8, :] = dst[a, nz + i, b, r:r + 8, :] + tmp[a, i, b, r:r + 8, :]
            return 0

        lax.fori_loop(0, nz, add, 0)


def last(info, f, g, gx, uf_in, ug_in, cz, cx, cm, cp, inv, ea, eb, filtered, adjoint, uf, ug, ub, e):
    nf, nz, nx, ny = f.shape
    nb = ny // BLOCK
    coef = (cz, cx, cm, cp, inv)
    pbase = jnp.where(info[0] == 0, 2 * nz, 0)
    copy = lane_copy(ny)
    edge = jnp.where(info[0] == 0, 2 * nz, nz - 1)
    for ref, base, q in ((ea, pbase, edge), (eb, 2 * nz - pbase, 3 * nz - 1 - edge)):
        e[...] = dot01(ref[...], copy)
        for a in range(nf):
            prolong(ub, e, a, a, 0, nx, nb)
            for i in range(nz):
                prolong(ub, e, nf + a * nz + i, a, 1 + i, nx, nb)
        for a in range(nf):
            for b in range(nb):
                for r in rows_of(True, nx):
                    uf[a, q, b, r:r + 8, :] = uf[a, q, b, r:r + 8, :] + ub[a, 0, b, r:r + 8, :]

        def add(i, _):
            for a in range(nf):
                for b in range(nb):
                    for r in rows_of(True, nx):
                        ug[a, base + i, b, r:r + 8, :] = ug[a, base + i, b, r:r + 8, :] + ub[a, 1 + i, b, r:r + 8, :]
            return 0

        lax.fori_loop(0, nz, add, 0)
    final(filtered, uf, f, coef, nz, nx)
    three(ug, ub, gx, coef, nz, nx)
    final(adjoint, ug, g, coef, nz, nx)


def coarse(info, rc, est, to_a, to_b, full, e0, e1, ck, cf, *, nf, nz, ng, nc, nb):
    half = nf
    nf = 2 * nf
    nr = ng * nc
    per = rc.shape[0] // ng
    lane = iota((8, BLOCK), 1)
    used = BLOCK // 4 * nb
    valid = lane < used
    zero = jnp.zeros((8, BLOCK), F32)
    for ref in (e0, e1, ck):
        for a in range(ref.shape[0]):
            ref[a, 0:8, :] = zero
            ref[a, 8 + nr:16 + nr, :] = zero
    at = info[5] * nc
    for k in range(nf * nz):
        for i in range(ng):
            row = i * per + (0 if k < half * nz else per // 2) + (k % (half * nz)) * nc
            full[k, i * nc:(i + 1) * nc, :] = rc[row:row + nc, :]
    for p in range(nz):
        for r in range(0, nr, 8):
            raw = full[p, r:r + 8, :]
            kc = zero
            for b in range(nb):
                column = jnp.broadcast_to(raw[:, BLOCK - nb + b:BLOCK - nb + b + 1], (8, BLOCK))
                kc = jnp.where(lane // (BLOCK // 4) == b, column, kc)
            ck[p, 8 + r:16 + r, :] = kc
            full[p, r:r + 8, :] = jnp.where(valid, raw, 0.0)
    for p in range(nz):
        dsum = zero
        rsum = [zero] * nf
        for r in range(0, nr, 8):
            s8 = slice(r, r + 8)
            k = ck[p, 8 + r:16 + r, :]
            xm = jnp.where(valid, 0.5 * (k + ck[p, 7 + r:15 + r, :]), 0.0)
            xp = jnp.where(valid, 0.5 * (k + ck[p, 9 + r:17 + r, :]), 0.0)
            ym = jnp.where(valid, 0.5 * (k + pltpu.roll(k, 1, 1)), 0.0)
            yp = jnp.where(valid, 0.5 * (k + pltpu.roll(k, BLOCK - 1, 1)), 0.0)
            d = 1.0 + xm + xp + ym + yp
            dsum = dsum + jnp.where(valid, d, 0.0)
            ci = jnp.where(valid, COARSE_RELAX / d, 0.0)
            cf[0, s8, :] = xm
            cf[1, s8, :] = xp
            cf[2, s8, :] = ym
            cf[3, s8, :] = yp
            cf[4, s8, :] = ci
            for a in range(nf):
                v = full[a * nz + p, s8, :]
                rsum[a] = rsum[a] + v
                e0[a, 8 + r:16 + r, :] = ci * v
        total = jnp.sum(dsum)
        shift = [jnp.sum(rsum[a]) / total for a in range(nf)]
        src, dst = e0, e1
        for n in range(COARSE_SWEEPS - 1):
            for r in range(0, nr, 8):
                s8 = slice(r, r + 8)
                c = [cf[i, s8, :] for i in range(5)]
                for a in range(nf):
                    v = src[a, 8 + r:16 + r, :]
                    s = c[0] * src[a, 7 + r:15 + r, :] + c[1] * src[a, 9 + r:17 + r, :]
                    s = s + c[2] * pltpu.roll(v, 1, 1) + c[3] * pltpu.roll(v, BLOCK - 1, 1)
                    v = (1.0 - COARSE_RELAX) * v + c[4] * (full[a * nz + p, s8, :] + s)
                    if n == COARSE_SWEEPS - 2:
                        v = jnp.where(valid, v + shift[a], 0.0)
                    dst[a, 8 + r:16 + r, :] = v
            src, dst = dst, src
        for a in range(nf):
            own = src[a, pl.ds(at + 7, 16), :]
            k = a * nz + p
            est[k * 16:(k + 1) * 16, :] = own
            if a >= half:
                m = (half + k - half * nz) * 16
                to_a[m:m + 16, :] = own
                to_b[m:m + 16, :] = own
            elif p in (0, nz - 1):
                m = slice(a * 16, (a + 1) * 16)

                @pl.when((info[0] == 0) == (p == nz - 1))
                def _():
                    to_a[m, :] = own

                @pl.when((info[0] == 0) == (p == 0))
                def _():
                    to_b[m, :] = own


def kappa_columns(width_class):
    table = jnp.array(WIDTH_TABLE, F32)
    table = table * table / 24.0
    hits = (width_class[..., None] == jnp.arange(CLASSES, dtype=jnp.int32)).astype(F32)
    kappa = jnp.sum(hits * table, axis=-1)
    nz, nx, nb = kappa.shape
    columns = jnp.transpose(kappa, (1, 0, 2)).reshape(nx, nz * nb)
    return jnp.pad(columns, ((0, 0), (0, BLOCK - nz * nb)))


def cycle(f, g, width_class):
    nf, nz, nx, ny = f.shape
    nb = ny // BLOCK
    nc = nx // 4
    nj, ng = lax.axis_size("jet"), lax.axis_size("grp")
    assert nz == DEEP and nj % 4 == 0 and ng % 2 == 0
    j, gi = lax.axis_index("jet"), lax.axis_index("grp")
    par = j % 2
    zp = (j // 2) % 2
    info = jnp.stack([par, (j == 0) * 1, (j == nj - 1) * 1, (gi == 0) * 1, (gi == ng - 1) * 1, gi, gi % 2, zp, (j < 2) * 1, (j >= nj - 2) * 1]).astype(jnp.int32)

    def both(pairs):
        return [p for a, b in pairs for p in ((a, b), (b, a))]

    swap = both([(i, i + 1) for i in range(0, nj, 2)])
    side = both([(i, (i + 1) % nj) for i in range(1, nj, 2)])
    inner = [pair for pair in side if abs(pair[0] - pair[1]) == 1]
    relay = [(i, (i + 2) % nj if i % 2 == 0 else (i - 2) % nj) for i in range(nj)]
    two_a = both([(i, (i + 2) % nj) for i in range(nj) if (i // 2) % 2 == 0])
    two_b = both([(i, (i + 2) % nj) for i in range(nj) if (i // 2) % 2 == 1])
    x_a = both([(i, i + 1) for i in range(0, ng, 2)])
    x_b = both([(i, (i + 1) % ng) for i in range(1, ng, 2)])

    def send(x, axis, perm):
        return lax.ppermute(x, axis, perm)

    pf = send(f, "jet", swap)
    ks = kappa_columns(width_class)
    near_k = [send(ks, "jet", swap), send(ks, "jet", side), send(ks, "jet", two_a), send(ks, "jet", two_b)]
    xs = (kappa_row(nf, nz) + 8, ny)
    to_a, to_b = call(pack_x, [xs, xs], [], info, f, g, smem=1)
    to_a, to_b, cols = call(
        functools.partial(pack_k, nf=nf, nz=nz, nb=nb), [xs, xs, (nx, BLOCK)], [],
        info, to_a, to_b, ks, *near_k, smem=1, alias={1: 0, 2: 1})
    xa, xb = send(to_a, "grp", x_a), send(to_b, "grp", x_b)
    ypack, low, high = call(functools.partial(pack_y, nf=nf, nz=nz), [(8 * nf * nz, ny), xs, xs], [], info, xa, xb, smem=1)
    py = send(ypack, "jet", swap)
    ry = send(ypack, "jet", side)
    pg = send(g, "jet", swap)
    rf = send(pf, "jet", relay)
    near = lax.dynamic_slice_in_dim(pg, (1 - par) * (nz - 1), 1, 1)
    rest = lax.dynamic_slice_in_dim(pg, par, nz - 1, 1)
    rn = send(near, "jet", relay)
    rr = send(rest, "jet", relay)

    xr = nx + 32
    deep = (nf, 3 * nz, nb, xr, BLOCK)
    co = (3 * nz, nb, xr, BLOCK)
    coefs = call(
        functools.partial(coefficients, nz=nz, nx=nx, nb=nb, at=kappa_row(nf, nz)),
        [(3 * nz + 1, nb, xr, BLOCK), co, co, co, co, (nz, nb, xr, BLOCK)], [(3 * nz + 2, nb, xr, BLOCK)],
        info, cols, low, high, smem=1)
    coef, diag = coefs[:5], coefs[5]
    rows = -(-nf * nz * nc // 8) * 8
    scratch = [(nb, nf * nz, nx, BLOCK), (rows, BLOCK)]
    u3, rcf = call(fwd_before, [deep, (rows, BLOCK)], [deep, deep] + scratch, info, f, pf, rf, low, high, py, ry, ks, *coef, diag, smem=1)
    (rc,) = call(adj_before, [(2 * rows, BLOCK)], [deep, deep] + scratch, info, g, pg, rn, low, high, rcf, *coef, diag, smem=1)
    whole = lax.all_gather(rc, "grp", axis=0, tiled=True)
    nr = ng * nc
    solve = [(2 * nf * nz, nr, BLOCK), (2 * nf, nr + 16, BLOCK), (2 * nf, nr + 16, BLOCK), (nz, nr + 16, BLOCK), (5, nr, BLOCK)]
    sent = (nf * (nz + 1) * 16, BLOCK)
    est, to_a, to_b = call(
        functools.partial(coarse, nf=nf, nz=nz, ng=ng, nc=nc, nb=nb),
        [(2 * nf * nz * 16, BLOCK), sent, sent], solve, info, whole, smem=1)
    ea, eb = send(to_a, "jet", swap), send(to_b, "jet", inner)
    uf, gx, ug = call(
        middle, [deep] * 3, [deep, (2 * nf * nz * 16, ny)],
        info, u3, g, pg, rn, rr, low, high, py, ry, coef[4], est, smem=1, alias={1: 0})
    filtered, adjoint, _, _ = call(
        last, [f.shape, g.shape, deep, deep], [deep, (nf * (nz + 1) * 16, ny)],
        info, f, g, gx, uf, ug, *coef, ea, eb, smem=1, alias={4: 2, 5: 3})
    return filtered, adjoint


def solution(mesh):
    placed = (P(None, "jet", "grp", None), P(None, "jet", "grp", None), P("jet", "grp", None))
    return jax.shard_map(
        cycle,
        mesh=mesh,
        in_specs=placed,
        out_specs=(P(None, "jet", "grp", None), P(None, "jet", "grp", None)),
        check_vma=False,
    )
```

```python
import functools

import jax
import jax.numpy as jnp
from jax import lax
from jax.experimental import pallas as pl
from jax.experimental.pallas import tpu as pltpu
from jax.sharding import PartitionSpec as P


BLOCK = 128
CLASSES = 8
COARSE_SWEEPS = 8
DEEP = 3
O = 16
WIDTH_TABLE = (2.5, 3.5, 4.5, 5.0, 6.0, 7.0, 8.5, 10.0)
RELAXATION = 0.8
COARSE_RELAX = 0.8
F32 = jnp.float32
BF16 = jnp.bfloat16


VM = pl.BlockSpec(memory_space=pltpu.VMEM)
SM = pl.BlockSpec(memory_space=pltpu.SMEM)


def padded(shape):
    n = 4
    for d in shape[:-2]:
        n *= d
    return n * (-(-shape[-2] // 8) * 8) * (-(-shape[-1] // BLOCK) * BLOCK)


def call(kernel, outs, scratch, *args, smem=0, cost=(1000000, 1000000)):
    specs = [SM] * smem + [VM] * (len(args) - smem)
    need = sum(map(padded, scratch))
    return pl.pallas_call(
        kernel,
        out_shape=[jax.ShapeDtypeStruct(s, F32) for s in outs],
        in_specs=specs,
        out_specs=[VM] * len(outs),
        scratch_shapes=[pltpu.VMEM(s, F32) for s in scratch],
        cost_estimate=pl.CostEstimate(flops=cost[0], bytes_accessed=cost[1], transcendentals=0),
        compiler_params=pltpu.CompilerParams(vmem_limit_bytes=need + (6 << 20)),
    )(*args)


def iota(shape, dim):
    return lax.broadcasted_iota(jnp.int32, shape, dim)


def pack_x(info, f, g, to_a, to_b):
    nf, nz, nx, _ = f.shape
    even = info[6] == 0
    for s, ref in enumerate((f, g)):
        for a in range(nf):
            for p in range(nz):
                at = ((s * nf + a) * nz + p) * DEEP
                first, last = ref[a, p, 0:DEEP, :], ref[a, p, nx - DEEP:nx, :]
                to_a[at:at + DEEP, :] = jnp.where(even, last, first)
                to_b[at:at + DEEP, :] = jnp.where(even, first, last)


def pack_k(info, ks, kp, ko, ka, kb, to_a, to_b, cols, *, nz, nb):
    nx = ks.shape[0]
    n = nz * nb
    lane = iota((nx, BLOCK), 1)

    def shift(x, at):
        return x if at % BLOCK == 0 else pltpu.roll(x, at % BLOCK, 1)

    def only(x, first, count, outside=None):
        keep = (lane >= first) & (lane < first + count)
        if outside is not None:
            keep = keep & (outside == 0)
        return jnp.where(keep, x, 0.0)

    up, far = info[0] == 0, info[7] == 0
    lo1, hi1 = jnp.where(up, ko[...], kp[...]), jnp.where(up, kp[...], ko[...])
    lo2, hi2 = jnp.where(far, kb[...], ka[...]), jnp.where(far, ka[...], kb[...])
    kall = shift(only(lo2, n - nb, nb, info[8]), nb - n) + shift(only(lo1, 0, n, info[1]), nb) + shift(only(ks[...], 0, n), nb + n)
    kall = kall + shift(only(hi1, 0, n, info[2]), nb + 2 * n) + shift(only(hi2, 0, nb, info[9]), nb + 3 * n)
    cols[...] = kall
    even = info[6] == 0
    first, last = kall[0:8, :], kall[nx - 8:nx, :]
    to_a[...] = jnp.where(even, last, first)
    to_b[...] = jnp.where(even, first, last)


def pack_y(info, xa, xb, out, low, high, *, nf, nz):
    even = info[6] == 0
    low[...] = jnp.where(even, xb[...], xa[...])
    high[...] = jnp.where(even, xa[...], xb[...])
    for a in range(2 * nf):
        for p in range(nz):
            src = (a * nz + p) * DEEP
            at = (a * nz + p) * 4
            out[at:at + 2, :] = low[src + 1:src + 3, :]
            out[at + 2:at + 4, :] = high[src:src + 2, :]


def dot01(x, m):
    h = x.astype(BF16)
    r = x - h.astype(F32)
    i = r.astype(BF16)
    j = (r - i.astype(F32)).astype(BF16)
    dot = functools.partial(jnp.dot, preferred_element_type=F32)
    return dot(h, m) + dot(i, m) + dot(j, m)


def lane_sum(b):
    l, m = iota((BLOCK, BLOCK), 0), iota((BLOCK, BLOCK), 1)
    return jnp.where((l + b * BLOCK) // 4 == m, 1.0 / 16.0, 0.0).astype(BF16)


def lane_copy(ny):
    m, l = iota((BLOCK, ny), 0), iota((BLOCK, ny), 1)
    return jnp.where(l // 4 == m, 1.0, 0.0).astype(BF16)


def around(v, nb, lane):
    rl = [pltpu.roll(x, 1, 1) for x in v]
    rr = [pltpu.roll(x, BLOCK - 1, 1) for x in v]
    left = [jnp.where(lane == 0, rl[i - 1] if i > 0 else 0.0, rl[i]) for i in range(nb)]
    right = [jnp.where(lane == BLOCK - 1, rr[i + 1] if i < nb - 1 else 0.0, rr[i]) for i in range(nb)]
    return left, right


def pull(src, co, p, r, a, nb, lane):
    czm, czp, cxm, cxp, cym, cyp = co
    v = [src[a, p, b, r:r + 8, :] for b in range(nb)]
    left, right = around(v, nb, lane)
    out = []
    for b in range(nb):
        s = czm[b] * src[a, p - 1, b, r:r + 8, :] + czp[b] * src[a, p + 1, b, r:r + 8, :]
        s = s + cxm[b] * src[a, p, b, r - 1:r + 7, :] + cxp[b] * src[a, p, b, r + 1:r + 9, :]
        s = s + cym[b] * left[b] + cyp[b] * right[b]
        out.append(s)
    return v, out


def coefs_at(coef, p, r, nb):
    cz, cx, cm, cp, _ = coef
    return (
        [cz[p, b, r:r + 8, :] for b in range(nb)],
        [cz[p + 1, b, r:r + 8, :] for b in range(nb)],
        [cx[p, b, r - 1:r + 7, :] for b in range(nb)],
        [cx[p, b, r:r + 8, :] for b in range(nb)],
        [cm[p, b, r:r + 8, :] for b in range(nb)],
        [cp[p, b, r:r + 8, :] for b in range(nb)],
    )


def rows_of(wide, nx):
    return range(O - 4, O + nx + 4, 8) if wide else range(O, O + nx, 8)


def sweep(dst, src, rhs, coef, first, count, stride, wide, nx):
    inv = coef[4]
    nf, nb = src.shape[0], src.shape[2]
    lane = iota((8, BLOCK), 1)

    def plane(i, _):
        p = first + i * stride
        for r in rows_of(wide, nx):
            co = coefs_at(coef, p, r, nb)
            w = [inv[p, b, r:r + 8, :] for b in range(nb)]
            for a in range(nf):
                v, s = pull(src, co, p, r, a, nb, lane)
                for b in range(nb):
                    dst[a, p, b, r:r + 8, :] = (1.0 - RELAXATION) * v[b] + w[b] * (rhs[a, p, b, r:r + 8, :] + s[b])
        return 0

    lax.fori_loop(0, count, plane, 0)


def three(ua, ub, rhs, coef, nz, nx, ahead=False):
    if ahead:
        sweep(ub, ua, rhs, coef, 2, 2, 1, True, nx)
        sweep(ub, ua, rhs, coef, 2 * nz - 1, 2, 1, True, nx)
    else:
        sweep(ub, ua, rhs, coef, 2, 2 * nz - 1, 1, True, nx)
    sweep(ub, ua, rhs, coef, 1, 2, 3 * nz - 3, False, nx)
    sweep(ua, ub, rhs, coef, nz, nz, 1, True, nx)
    sweep(ua, ub, rhs, coef, nz - 1, 2, nz + 1, False, nx)


def final(dst, src, rhs, coef, nz, nx, which):
    inv = coef[4]
    nf, nb = src.shape[0], src.shape[2]
    lane = iota((8, BLOCK), 1)

    def plane(i):
        p = nz + i
        for r in rows_of(False, nx):
            co = coefs_at(coef, p, r, nb)
            w = [inv[p, b, r:r + 8, :] for b in range(nb)]
            for a in range(nf):
                v, s = pull(src, co, p, r, a, nb, lane)
                for b in range(nb):
                    c = slice(b * BLOCK, (b + 1) * BLOCK)
                    q = r - O
                    dst[a, i, q:q + 8, c] = (1.0 - RELAXATION) * v[b] + w[b] * (rhs[a, i, q:q + 8, c] + s[b])
        return 0

    for i in which:
        plane(i)


def restrict_residual(out, base, src, rhs, coef, diag, tmp, parts, nz, nx):
    nf, nb = src.shape[0], src.shape[2]
    lane = iota((8, BLOCK), 1)

    def plane(i, _):
        p = nz + i
        for r in rows_of(False, nx):
            co = coefs_at(coef, p, r, nb)
            d = [diag[p, b, r:r + 8, :] for b in range(nb)]
            for a in range(nf):
                v, s = pull(src, co, p, r, a, nb, lane)
                for b in range(nb):
                    c = slice(b * BLOCK, (b + 1) * BLOCK)
                    q = r - O
                    tmp[b, a * nz + i, q:q + 8, :] = rhs[a, i, q:q + 8, c] - d[b] * v[b] + s[b]
        return 0

    lax.fori_loop(0, nz, plane, 0)
    nc = nx // 4
    total = None
    for b in range(nb):
        for k in range(nf * nz):
            parts[k * nc:(k + 1) * nc, :] = sum(tmp[b, k, pl.ds(j, nc, stride=4), :] for j in range(4))
        dot = dot01(parts[...], lane_sum(b))
        total = dot if total is None else total + dot
    out[base:base + total.shape[0], :] = total


def coarse_kappa(out, ks, tmp, nz, nx, nb):
    nc = nx // 4
    tmp[0, 0, 0:nx, :] = ks[...]
    kc = sum(tmp[0, 0, pl.ds(j, nc, stride=4), :] for j in range(4)) * (1.0 / 64.0)
    for p in range(nz):
        l, m = iota((BLOCK, BLOCK), 0), iota((BLOCK, BLOCK), 1)
        pick = jnp.where((l - p * nb == m - (BLOCK - nb)) & (m >= BLOCK - nb), 1.0, 0.0).astype(BF16)
        rows = slice(p * nc, (p + 1) * nc)
        out[rows, :] = out[rows, :] + dot01(kc, pick)


def coefficients(info, cols, xa, xb, cz, cx, cm, cp, inv, diag, kap, *, nz, nx, nb):
    first_j, last_j, first_g, last_g = (info[i] for i in range(1, 5))
    even = info[6] == 0
    below = jnp.where(first_g == 1, 0.0, jnp.where(even, xb[4:8, :], xa[4:8, :]))
    above = jnp.where(last_g == 1, 0.0, jnp.where(even, xa[0:4, :], xb[0:4, :]))
    for row, value in ((O - 4, below), (O, cols[...]), (O + nx, above)):
        n = value.shape[0]
        for p in range(3 * nz + 2):
            for b in range(nb):
                c = p * nb + b
                kap[p, b, row:row + n, :] = jnp.broadcast_to(value[:, c:c + 1], (n, BLOCK))
    lane = iota((8, BLOCK), 1)

    def cplane(p, _):
        out = ((first_j == 1) & (p < nz)) | ((last_j == 1) & (p >= 2 * nz))
        for r in rows_of(True, nx):
            row = iota((8, BLOCK), 0) + (r - O)
            here = jnp.where(((row < 0) & (first_g == 1)) | ((row >= nx) & (last_g == 1)) | out, 0.0, RELAXATION)
            s8 = slice(r, r + 8)
            k = [kap[p + 1, b, s8, :] for b in range(nb)]
            for b in range(nb):
                below, above = kap[p, b, s8, :], kap[p + 2, b, s8, :]
                before, behind = kap[p + 1, b, r - 1:r + 7, :], kap[p + 1, b, r + 1:r + 9, :]
                ym = jnp.where(lane == 0, 0.5 * (k[b] + k[b - 1]) if b > 0 else 0.5 * k[b], k[b])
                yp = jnp.where(lane == BLOCK - 1, 0.5 * (k[b] + k[b + 1]) if b < nb - 1 else 0.5 * k[b], k[b])
                cz[p, b, s8, :] = 0.5 * (below + k[b])
                cx[p, b, s8, :] = 0.5 * (k[b] + behind)
                cm[p, b, s8, :] = ym
                cp[p, b, s8, :] = yp
                d = (1.0 + 2.0 * k[b]) + 0.5 * ((below + above) + (before + behind)) + (ym + yp)
                inv[p, b, s8, :] = here / d
                diag[p, b, s8, :] = d
        return 0

    lax.fori_loop(0, 3 * nz, cplane, 0)


def lay(dst, ref, a, p, q, rows, lo_row, hi_row, nx, nb, field=None):
    width, _, pack = rows
    for b in range(nb):
        c = slice(b * BLOCK, (b + 1) * BLOCK)
        dst[a, q, b, O:O + nx, :] = ref[a if field is None else field, p, :, c]
        if pack is not None:
            dst[a, q, b, O - width:O, :] = pack[0][lo_row:lo_row + width, c]
            dst[a, q, b, O + nx:O + nx + width, :] = pack[1][hi_row:hi_row + width, c]


def ends(low, high, s, a, p, nf, nz):
    at = ((s * nf + a) * nz + p) * DEEP
    return (DEEP, None, (low, high)), at, at


def corners(pack, s, a, p, nf, nz):
    at = ((s * nf + a) * nz + p) * 4
    return (2, None, (pack, pack)), at, at + 2


def start(dst, own, inv, p, nx, nb, nf):
    for a in range(nf):
        for b in range(nb):
            for r in rows_of(True, nx):
                dst[a, p, b, r:r + 8, :] = inv[p, b, r:r + 8, :] * own[a, p, b, r:r + 8, :]


def fwd_before(info, f, pfa, pfb, rfa, rfb, low, high, py, ry, ks, cz, cx, cm, cp, inv, diag, u3, rc, fx, ub, tmp, parts):
    nf, nz, nx, ny = f.shape
    nb = ny // BLOCK
    par = info[0]
    pbase = jnp.where(par == 0, 2 * nz, 0)
    rbase = 2 * nz - pbase
    for a in range(nf):
        for p in range(nz):
            lay(fx, f, a, p, nz + p, *ends(low, high, 0, a, p, nf, nz), nx, nb)
            pf, rf, at = (pfa, rfa, a) if a < nf - 1 else (pfb, rfb, 0)
            lay(fx, pf, a, p, pbase + p, *corners(py, 0, a, p, nf, nz), nx, nb, at)
            lay(fx, rf, a, p, rbase + p, *corners(ry, 0, a, p, nf, nz), nx, nb, at)
    coef = (cz, cx, cm, cp, inv)

    def one(p, _):
        start(u3, fx, inv, p, nx, nb, nf)
        return 0

    lax.fori_loop(0, 3 * nz, one, 0)
    three(u3, ub, fx, coef, nz, nx)
    restrict_residual(rc, 0, u3, f, coef, diag, tmp, parts, nz, nx)
    coarse_kappa(rc, ks, tmp, nz, nx, nb)


def adj_before(info, g, pgn, rn, low, high, rcf, cz, cx, cm, cp, inv, diag, rc, gx, ua, tmp, parts):
    nf, nz, nx, ny = g.shape
    nb = ny // BLOCK
    par = info[0]
    pp = jnp.where(par == 0, 2 * nz, nz - 1)
    rp = 3 * nz - 1 - pp
    none = (0, None, None)
    for a in range(nf):
        for p in range(nz):
            lay(gx, g, a, p, nz + p, *ends(low, high, 1, a, p, nf, nz), nx, nb)
        lay(gx, pgn, a, par, pp, none, 0, 0, nx, nb)
        lay(gx, rn, a, 0, rp, none, 0, 0, nx, nb)

    def one(p, _):
        start(ua, gx, inv, p, nx, nb, nf)
        return 0

    lax.fori_loop(nz - 1, 2 * nz + 1, one, 0)
    n = rcf.shape[0]
    rc[0:n, :] = rcf[...]
    restrict_residual(rc, n, ua, g, (cz, cx, cm, cp, inv), diag, tmp, parts, nz, nx)


def prolong(dst, e, k, a, q, nx, nb):
    nc = nx // 4
    for b in range(nb):
        part = e[k * 16:k * 16 + nc + 2, b * BLOCK:(b + 1) * BLOCK]
        for j in range(4):
            dst[a, q, b, pl.ds(O - 4 + j, nc + 2, stride=4), :] = part


def add_rows(dst, src, other, p, q, nx):
    for a in range(src.shape[0]):
        for b in range(src.shape[2]):
            for r in rows_of(True, nx):
                dst[a, p, b, r:r + 8, :] = src[a, p, b, r:r + 8, :] + other[a, q, b, r:r + 8, :]


def copy_rows(dst, src, p, nx):
    for a in range(src.shape[0]):
        for b in range(src.shape[2]):
            for r in rows_of(True, nx):
                dst[a, p, b, r:r + 8, :] = src[a, p, b, r:r + 8, :]


def middle(info, u3, f, g, pgn, pgm, rn, rr, rm, low, high, py, ry, cz, cx, cm, cp, inv, est, uf, gx, ug, ub, filtered, tmp, e):
    nf, nz, nx, ny = g.shape
    nb = ny // BLOCK
    par = info[0]
    pbase = jnp.where(par == 0, 2 * nz, 0)
    rbase = 2 * nz - pbase
    near = jnp.where(par == 0, nz - 1, 0)
    none = (0, None, None)
    for a in range(nf):
        for p in range(nz):
            lay(gx, g, a, p, nz + p, *ends(low, high, 1, a, p, nf, nz), nx, nb)
            ref, at = (pgm, p - 1) if 0 < p < nz - 1 else (pgn, min(p, 1))
            lay(gx, ref, a, at, pbase + p, *corners(py, 1, a, p, nf, nz), nx, nb)
        lay(gx, rn, a, 0, rbase + near, none, 0, 0, nx, nb)
        lay(gx, rr, a, 0, rbase + nz - 1 - near, none, 0, 0, nx, nb)
        for p in range(1, nz - 1):
            lay(gx, rm, a, p - 1, rbase + p, none, 0, 0, nx, nb)
        for p in range(nz):
            (width, _, pack), lo_row, hi_row = corners(ry, 1, a, p, nf, nz)
            for b in range(nb):
                c = slice(b * BLOCK, (b + 1) * BLOCK)
                gx[a, rbase + p, b, O - width:O, :] = ry[lo_row:lo_row + width, c]
                gx[a, rbase + p, b, O + nx:O + nx + width, :] = ry[hi_row:hi_row + width, c]

    def one(p, _):
        start(ug, gx, inv, p, nx, nb, nf)
        return 0

    lax.fori_loop(0, 3 * nz, one, 0)
    e[...] = dot01(est[...], lane_copy(ny))
    for s, (dst, src) in enumerate(((uf, u3), (ug, ug))):
        for a in range(nf):
            for i in range(nz):
                prolong(tmp, e, (s * nf + a) * nz + i, a, i, nx, nb)
        for i in range(nz):
            add_rows(dst, src, tmp, nz + i, i, nx)
    for p in (nz - 1, 2 * nz):
        copy_rows(uf, u3, p, nx)
    coef = (cz, cx, cm, cp, inv)
    final(filtered, uf, f, coef, nz, nx, range(1, nz - 1))
    sweep(ub, ug, gx, coef, nz + 1, nz - 2, 1, True, nx)


def last(info, f, g, gx, uf_in, ug_in, ub_in, filtered_in, cz, cx, cm, cp, inv, ea, eb, filtered, adjoint, uf, ug, ub, tmp, e):
    nf, nz, nx, ny = f.shape
    nb = ny // BLOCK
    coef = (cz, cx, cm, cp, inv)
    pbase = jnp.where(info[0] == 0, 2 * nz, 0)
    copy = lane_copy(ny)
    edge = jnp.where(info[0] == 0, 2 * nz, nz - 1)
    for p in range(nz, 2 * nz):
        copy_rows(uf, uf_in, p, nx)
        copy_rows(ug, ug_in, p, nx)
    for p in range(nz + 1, 2 * nz - 1):
        copy_rows(ub, ub_in, p, nx)
        filtered[:, p - nz, :, :] = filtered_in[:, p - nz, :, :]
    for ref, base, q in ((ea, pbase, edge), (eb, 2 * nz - pbase, 3 * nz - 1 - edge)):
        e[...] = dot01(ref[...], copy)
        for a in range(nf):
            prolong(tmp, e, a, a, 0, nx, nb)
            for i in range(nz):
                prolong(tmp, e, nf + a * nz + i, a, 1 + i, nx, nb)
        add_rows(uf, uf_in, tmp, q, 0, nx)
        for i in range(nz):
            add_rows(ug, ug_in, tmp, base + i, 1 + i, nx)
    final(filtered, uf, f, coef, nz, nx, (0, nz - 1))
    three(ug, ub, gx, coef, nz, nx, True)
    final(adjoint, ug, g, coef, nz, nx, range(nz))


def coarse(info, rc, est, to_a, to_b, full, e0, e1, ck, cf, *, nf, nz, ng, nc, nb):
    half = nf
    nf = 2 * nf
    nr = ng * nc
    per = rc.shape[0] // ng
    lane = iota((8, BLOCK), 1)
    used = BLOCK // 4 * nb
    valid = lane < used
    zero = jnp.zeros((8, BLOCK), F32)
    for ref in (e0, e1, ck):
        for a in range(ref.shape[0]):
            ref[a, 0:8, :] = zero
            ref[a, 8 + nr:16 + nr, :] = zero
    at = info[5] * nc
    for k in range(nf * nz):
        for i in range(ng):
            row = i * per + (0 if k < half * nz else per // 2) + (k % (half * nz)) * nc
            full[k, i * nc:(i + 1) * nc, :] = rc[row:row + nc, :]
    for p in range(nz):
        for r in range(0, nr, 8):
            raw = full[p, r:r + 8, :]
            kc = zero
            for b in range(nb):
                column = jnp.broadcast_to(raw[:, BLOCK - nb + b:BLOCK - nb + b + 1], (8, BLOCK))
                kc = jnp.where(lane // (BLOCK // 4) == b, column, kc)
            ck[p, 8 + r:16 + r, :] = kc
            full[p, r:r + 8, :] = jnp.where(valid, raw, 0.0)
    for p in range(nz):
        dsum = zero
        rsum = [zero] * nf
        for r in range(0, nr, 8):
            s8 = slice(r, r + 8)
            k = ck[p, 8 + r:16 + r, :]
            xm = jnp.where(valid, 0.5 * (k + ck[p, 7 + r:15 + r, :]), 0.0)
            xp = jnp.where(valid, 0.5 * (k + ck[p, 9 + r:17 + r, :]), 0.0)
            ym = jnp.where(valid, 0.5 * (k + pltpu.roll(k, 1, 1)), 0.0)
            yp = jnp.where(valid, 0.5 * (k + pltpu.roll(k, BLOCK - 1, 1)), 0.0)
            d = 1.0 + xm + xp + ym + yp
            dsum = dsum + jnp.where(valid, d, 0.0)
            ci = jnp.where(valid, COARSE_RELAX / d, 0.0)
            cf[0, s8, :] = xm
            cf[1, s8, :] = xp
            cf[2, s8, :] = ym
            cf[3, s8, :] = yp
            cf[4, s8, :] = ci
            for a in range(nf):
                v = full[a * nz + p, s8, :]
                rsum[a] = rsum[a] + v
                e0[a, 8 + r:16 + r, :] = ci * v
        total = jnp.sum(dsum)
        shift = [jnp.sum(rsum[a]) / total for a in range(nf)]
        src, dst = e0, e1
        for n in range(COARSE_SWEEPS - 1):
            for r in range(0, nr, 8):
                s8 = slice(r, r + 8)
                c = [cf[i, s8, :] for i in range(5)]
                for a in range(nf):
                    v = src[a, 8 + r:16 + r, :]
                    s = c[0] * src[a, 7 + r:15 + r, :] + c[1] * src[a, 9 + r:17 + r, :]
                    s = s + c[2] * pltpu.roll(v, 1, 1) + c[3] * pltpu.roll(v, BLOCK - 1, 1)
                    v = (1.0 - COARSE_RELAX) * v + c[4] * (full[a * nz + p, s8, :] + s)
                    if n == COARSE_SWEEPS - 2:
                        v = jnp.where(valid, v + shift[a], 0.0)
                    dst[a, 8 + r:16 + r, :] = v
            src, dst = dst, src
        for a in range(nf):
            own = src[a, pl.ds(at + 7, 16), :]
            k = a * nz + p
            est[k * 16:(k + 1) * 16, :] = own
            if a >= half:
                m = (half + k - half * nz) * 16
                to_a[m:m + 16, :] = own
                to_b[m:m + 16, :] = own
            elif p in (0, nz - 1):
                m = slice(a * 16, (a + 1) * 16)

                @pl.when((info[0] == 0) == (p == nz - 1))
                def _():
                    to_a[m, :] = own

                @pl.when((info[0] == 0) == (p == 0))
                def _():
                    to_b[m, :] = own


def kappa_columns(width_class):
    table = jnp.array(WIDTH_TABLE, F32)
    table = table * table / 24.0
    hits = (width_class[..., None] == jnp.arange(CLASSES, dtype=jnp.int32)).astype(F32)
    kappa = jnp.sum(hits * table, axis=-1)
    nz, nx, nb = kappa.shape
    columns = jnp.transpose(kappa, (1, 0, 2)).reshape(nx, nz * nb)
    return jnp.pad(columns, ((0, 0), (0, BLOCK - nz * nb)))


def cycle(f, g, width_class):
    nf, nz, nx, ny = f.shape
    nb = ny // BLOCK
    nc = nx // 4
    nj, ng = lax.axis_size("jet"), lax.axis_size("grp")
    assert nz == DEEP and nj % 4 == 0 and ng % 4 == 0 and ng & (ng - 1) == 0
    j, gi = lax.axis_index("jet"), lax.axis_index("grp")
    par = j % 2
    zp = (j // 2) % 2
    info = jnp.stack([par, (j == 0) * 1, (j == nj - 1) * 1, (gi == 0) * 1, (gi == ng - 1) * 1, gi, gi % 2, zp, (j < 2) * 1, (j >= nj - 2) * 1]).astype(jnp.int32)

    def both(pairs):
        return [p for a, b in pairs for p in ((a, b), (b, a))]

    swap = both([(i, i + 1) for i in range(0, nj, 2)])
    side = both([(i, (i + 1) % nj) for i in range(1, nj, 2)])
    inner = [pair for pair in side if abs(pair[0] - pair[1]) == 1]
    relay = [(i, (i + 2) % nj if i % 2 == 0 else (i - 2) % nj) for i in range(nj)]
    two_a = both([(i, (i + 2) % nj) for i in range(nj) if (i // 2) % 2 == 0])
    two_b = both([(i, (i + 2) % nj) for i in range(nj) if (i // 2) % 2 == 1])
    x_a = both([(i, i + 1) for i in range(0, ng, 2)])
    x_b = both([(i, (i + 1) % ng) for i in range(1, ng, 2)])

    def send(x, axis, perm):
        return lax.ppermute(x, axis, perm)

    pfa, pfb = send(f[:nf - 1], "jet", swap), send(f[nf - 1:], "jet", swap)
    ks = kappa_columns(width_class)
    near_k = [send(ks, "jet", swap), send(ks, "jet", side), send(ks, "jet", two_a), send(ks, "jet", two_b)]
    xs = (-(-2 * nf * nz * DEEP // 8) * 8, ny)
    to_a, to_b = call(pack_x, [xs, xs], [], info, f, g, smem=1)
    xa, xb = send(to_a, "grp", x_a), send(to_b, "grp", x_b)
    ypack, low, high = call(functools.partial(pack_y, nf=nf, nz=nz), [(8 * nf * nz, ny), xs, xs], [], info, xa, xb, smem=1)
    py = send(ypack, "jet", swap)
    ry = send(ypack, "jet", side)
    outer = jnp.concatenate([g[:, :1], g[:, nz - 1:]], axis=1)
    mids = g[:, 1:nz - 1]
    pgn, pgm = send(outer, "jet", swap), send(mids, "jet", swap)
    k_to_a, k_to_b, cols = call(
        functools.partial(pack_k, nz=nz, nb=nb), [(8, BLOCK), (8, BLOCK), (nx, BLOCK)], [], info, ks, *near_k, smem=1)
    kxa, kxb = send(k_to_a, "grp", x_a), send(k_to_b, "grp", x_b)
    rfa, rfb = send(pfa, "jet", relay), send(pfb, "jet", relay)
    near = lax.dynamic_slice_in_dim(pgn, 1 - par, 1, 1)
    rest = lax.dynamic_slice_in_dim(pgn, par, 1, 1)
    rn = send(near, "jet", relay)
    rr, rm = send(rest, "jet", relay), send(pgm, "jet", relay)

    xr = nx + 32
    deep = (nf, 3 * nz, nb, xr, BLOCK)
    co = (3 * nz, nb, xr, BLOCK)
    coefs = call(
        functools.partial(coefficients, nz=nz, nx=nx, nb=nb),
        [co] * 6, [(3 * nz + 2, nb, xr, BLOCK)],
        info, cols, kxa, kxb, smem=1)
    coef, diag = coefs[:5], coefs[5]
    rows = -(-nf * nz * nc // 8) * 8
    scratch = [(nb, nf * nz, nx, BLOCK), (rows, BLOCK)]
    u3, rcf = call(fwd_before, [deep, (rows, BLOCK)], [deep, deep] + scratch, info, f, pfa, pfb, rfa, rfb, low, high, py, ry, ks, *coef, diag, smem=1)
    (rc,) = call(adj_before, [(2 * rows, BLOCK)], [deep, deep] + scratch, info, g, pgn, rn, low, high, rcf, *coef, diag, smem=1)
    whole = lax.all_gather(rc, "grp", axis=0, tiled=True)
    nr = ng * nc
    solve = [(2 * nf * nz, nr, BLOCK), (2 * nf, nr + 16, BLOCK), (2 * nf, nr + 16, BLOCK), (nz, nr + 16, BLOCK), (5, nr, BLOCK)]
    sent = (nf * (nz + 1) * 16, BLOCK)
    est, to_a, to_b = call(
        functools.partial(coarse, nf=nf, nz=nz, ng=ng, nc=nc, nb=nb),
        [(2 * nf * nz * 16, BLOCK), sent, sent], solve, info, whole, smem=1)
    ea, eb = send(to_a, "jet", swap), send(to_b, "jet", inner)
    uf, gx, ug, ub, done = call(
        middle, [deep] * 4 + [f.shape], [(nf, nz, nb, xr, BLOCK), (2 * nf * nz * 16, ny)],
        info, u3, f, g, pgn, pgm, rn, rr, rm, low, high, py, ry, *coef, est, smem=1)
    filtered, adjoint = call(
        last, [f.shape, g.shape], [deep] * 3 + [(nf, nz + 1, nb, xr, BLOCK), (nf * (nz + 1) * 16, ny)],
        info, f, g, gx, uf, ug, ub, done, *coef, ea, eb, smem=1)
    return filtered, adjoint


def solution(mesh):
    placed = (P(None, "jet", "grp", None), P(None, "jet", "grp", None), P("jet", "grp", None))
    return jax.shard_map(
        cycle,
        mesh=mesh,
        in_specs=placed,
        out_specs=(P(None, "jet", "grp", None), P(None, "jet", "grp", None)),
        check_vma=False,
    )
```
